32 devices in a mesh: gx: 2 (over core), gy: 4 (over y, x), gz: 4 (over z).
Axes of the slice: x: 2, y: 2, z: 4, core: 2. Of those that a mesh axis runs over, the one named last changes fastest.
Arguments:
- features: bfloat16 [4096, 512], P(('gx', 'gy', 'gz')), may hold values from -6 to 6
- halo_index: int32 [3072], P(('gx', 'gy', 'gz')), may hold values from 0 to 127
- edge_src: int32 [128, 384], P(('gx', 'gy', 'gz')), may hold values from 0 to 2623
- edge_dst: int32 [128, 384], P(('gx', 'gy', 'gz')), may hold values from 0 to 127
- edge_count: int32 [128], P(('gx', 'gy', 'gz')), may hold values from 48 to 384, as said below
- edge_basis: bfloat16 [49152, 128], P(('gx', 'gy', 'gz')), may hold values from -6 to 6
- w_edge_in: bfloat16 [4, 1152, 1024], P('gz'), may hold values from -0.1875 to 0.1875
- w_edge_out: bfloat16 [4, 1024, 512], P('gz'), may hold values from -0.1875 to 0.1875
- w_update: bfloat16 [512, 512], replicated, may hold values from -0.25 to 0.25
Outputs:
- new_features: bfloat16 [4096, 512], P(('gx', 'gy', 'gz'))
- halo_next: bfloat16 [832, 96, 512], P(('gx', 'gy', 'gz'))
The draws below stay inside these ranges and needn't reach their ends.
Inputs may be any that keep to these rules, and one draw needn't show every extreme that they name: The first edge_count slots of a domain's 384 slots for a species pair are live; in every draw some species pair has all 384 slots live in every domain of one gz group.
All inputs are finite; a program needn't handle non-finite values.
Results may differ from the reference program's by a relative error of at most 0.0051.
Values may be sent and summed in bfloat16 or wider, within the bound.
A program may use at most 128 MiB of HBM per device.

```python
import jax
import jax.numpy as jnp
from jax import lax

D = 512
HID = 1024
RB = 128
ATOM_DEV = 128
CAP = 384
HALO = 96
TABLE = 2624
TYPES = 4
ATOMS = 4096
N_GX = 2
N_GY = 4
N_GZ = 4
DEVICES = 32


def draw_edge_count(key, part):
    key_counts, key_group, key_helper = jax.random.split(key, 3)
    counts = jax.random.randint(key_counts, (DEVICES, N_GZ), CAP // 8, CAP + 1)
    group = jax.random.randint(key_group, (), 0, DEVICES // N_GZ)
    helper = jax.random.randint(key_helper, (), 0, N_GZ)
    rows = lax.broadcasted_iota(jnp.int32, (DEVICES, N_GZ), 0) // N_GZ
    columns = lax.broadcasted_iota(jnp.int32, (DEVICES, N_GZ), 1)
    filled = (rows == group) & (columns == helper)
    return jnp.where(filled, CAP, counts).reshape(DEVICES * N_GZ).astype(jnp.int32)


def set_ends(drawn, own_key, least, top_value):
    dims = drawn.shape
    spot = [jax.random.randint(jax.random.fold_in(own_key, axis), (), 0, dims[axis]) for axis in range(len(dims))]
    drawn = drawn.at[tuple(spot)].set(least)
    longest = dims.index(max(dims))
    spot[longest] = (spot[longest] + 1) % dims[longest]
    return drawn.at[tuple(spot)].set(top_value)


def levels(key, dims, cuts, smallest, top_value):
    def one(position, parts):
        draws = jax.random.uniform(jax.random.fold_in(jax.random.fold_in(key, 6), position), (parts,), jnp.float32, smallest / len(cuts), top_value / len(cuts))
        return jnp.repeat(jnp.exp(draws), dims[position] // parts).reshape((-1,) + (1,) * (len(dims) - position - 1))

    factor_of = one(*cuts[0])
    for cut in cuts[1:]:
        factor_of = factor_of * one(*cut)
    return factor_of


def normal_values(key, dims, width, reach, cuts=(), held_as=jnp.bfloat16):
    result = jax.random.normal(key, dims, jnp.float32) * width
    if len(cuts) > 0:
        result = levels(key, dims, cuts, -0.22, 0.18) * result
    return jnp.clip(result, min=-reach, max=reach).astype(held_as)


def setup_inputs(seed: int = 0) -> dict:
    key_of = jax.random.split(jax.random.key(seed), 10)
    features = normal_values(key_of[0], (ATOMS, D), 1.0, 6.0, ((0, 32),))
    halo_index = set_ends(jax.random.randint(key_of[1], (DEVICES * HALO,), 0, ATOM_DEV), jax.random.fold_in(key_of[1], 1), 0, ATOM_DEV - 1).astype(jnp.int32)
    edge_src = set_ends(jax.random.randint(key_of[2], (DEVICES * N_GZ, CAP), 0, TABLE), jax.random.fold_in(key_of[2], 1), 0, TABLE - 1).astype(jnp.int32)
    edge_dst = set_ends(jax.random.randint(key_of[3], (DEVICES * N_GZ, CAP), 0, ATOM_DEV), jax.random.fold_in(key_of[3], 1), 0, ATOM_DEV - 1).astype(jnp.int32)
    edge_count = draw_edge_count(jax.random.fold_in(key_of[9], 71), 0)
    edge_basis = normal_values(key_of[5], (DEVICES * N_GZ * CAP, RB), 1.0, 6.0, ((0, 32),))
    w_edge_in = normal_values(key_of[6], (TYPES, 2 * D + RB, HID), (2 * D + RB) ** -0.5, 0.1875, ((0, 4),))
    w_edge_out = normal_values(key_of[7], (TYPES, HID, D), HID ** -0.5, 0.1875, ((0, 4),))
    w_update = normal_values(key_of[8], (D, D), D ** -0.5, 0.25)
    return dict(features=features, halo_index=halo_index, edge_src=edge_src, edge_dst=edge_dst, edge_count=edge_count, edge_basis=edge_basis, w_edge_in=w_edge_in, w_edge_out=w_edge_out, w_update=w_update)


def neighbour_blocks(values, halo_index):
    boundary = jnp.take_along_axis(values, halo_index.reshape(DEVICES, HALO)[:, :, None], axis=1)
    boundary = boundary.reshape(N_GX, N_GY, N_GZ, HALO, D)
    blocks = []
    for shift_x in range(3):
        for shift_y in range(3):
            for shift_z in range(3):
                if shift_x == 1 and shift_y == 1 and (shift_z == 1):
                    continue
                blocks.append(jnp.roll(boundary, (1 - shift_x, 1 - shift_y, 1 - shift_z), axis=(0, 1, 2)))
    return jnp.stack(blocks, axis=3).reshape(DEVICES, 26 * HALO, D)

def reference(features, halo_index, edge_src, edge_dst, edge_count, edge_basis, w_edge_in, w_edge_out, w_update):
    own_rows = features.reshape(DEVICES, ATOM_DEV, D)
    table = jnp.concatenate([own_rows, neighbour_blocks(own_rows, halo_index)], axis=1)
    first_layer = w_edge_in.astype(jnp.float32)
    second_layer = w_edge_out.astype(jnp.float32)
    sources = edge_src.reshape(DEVICES, N_GZ, CAP)
    targets = edge_dst.reshape(DEVICES, N_GZ, CAP)
    counts = edge_count.reshape(DEVICES, N_GZ)
    basis = edge_basis.reshape(DEVICES, N_GZ, CAP, RB)

    def one_domain(items):
        table_rows, src_rows, dst_rows, count_rows, basis_rows = items
        inputs = jnp.concatenate([table_rows[src_rows], table_rows[dst_rows], basis_rows], axis=-1).astype(jnp.float32)
        pre = jnp.einsum('jck,jkh->jch', inputs, first_layer)
        hidden = lax.optimization_barrier(jax.nn.silu(pre).astype(jnp.bfloat16)).astype(jnp.float32)
        message = jnp.einsum('jch,jhd->jcd', hidden, second_layer).astype(jnp.bfloat16)
        message = lax.optimization_barrier(message).astype(jnp.float32)
        live = jnp.arange(CAP, dtype=jnp.int32)[None, :] < count_rows[:, None]
        message = jnp.where(live[:, :, None], message, jnp.float32(0.0))
        return jax.ops.segment_sum(message.reshape(-1, D), dst_rows.reshape(-1), num_segments=ATOM_DEV)
    aggregate = lax.map(one_domain, (table, sources, targets, counts, basis))
    normed = aggregate * lax.rsqrt(lax.optimization_barrier(jnp.mean(aggregate * aggregate, axis=-1, keepdims=True)) + 1e-05)
    normed = normed.astype(jnp.bfloat16).reshape(ATOMS, D)
    update = jnp.dot(normed, w_update, preferred_element_type=jnp.float32)
    new_features = (features.astype(jnp.float32) + update).astype(jnp.bfloat16)
    halo_next = neighbour_blocks(new_features.reshape(DEVICES, ATOM_DEV, D), halo_index)
    return (new_features, halo_next.reshape(DEVICES * 26, HALO, D))
```

```python
import functools

import jax
import jax.numpy as jnp
from jax import lax
from jax.experimental import pallas as pl
from jax.experimental.pallas import tpu as pltpu
from jax.sharding import PartitionSpec as P

AXES = ("gx", "gy", "gz")
MESH = pl.DeviceIdType.MESH


class Place:
    def __init__(self, sizes):
        self.nx, self.ny, self.nz = sizes
        self.x, self.y, self.z = (lax.axis_index(name) for name in AXES)
        x, y, z = self.x, self.y, self.z
        self.first = (x, y + 1 - 2 * lax.rem(y, 2), z)
        self.second = (x, lax.rem(y + 2, 4), z)
        self.b_first = 2 - 2 * lax.rem(y, 2)
        self.b_second = 2 * lax.rem(y, 2)
        self.siblings = [(lax.rem(x + 1, self.nx), y, z)]
        if self.nx > 2:
            self.siblings.append((lax.rem(x + self.nx - 1, self.nx), y, z))

    def along_z(self, step):
        return (self.x, self.y, lax.rem(self.z + step + self.nz, self.nz))

    def sibling_slot(self, index):
        return 1 if self.nx == 2 else 2 - index

    def greet(self):
        self.barrier = pltpu.get_barrier_semaphore()
        partners = [self.along_z(step) for step in range(1, self.nz)]
        partners += [self.first, self.second] + self.siblings
        for partner in partners:
            pl.semaphore_signal(self.barrier, inc=1, device_id=partner, device_id_type=MESH)
        self.partners = len(partners)

    def meet(self):
        pl.semaphore_wait(self.barrier, self.partners)


def remote(source, target, send, receive, device):
    return pltpu.make_async_remote_copy(
        src_ref=source,
        dst_ref=target,
        send_sem=send,
        recv_sem=receive,
        device_id=device,
        device_id_type=MESH,
    )


def layer_kernel(sizes, f_hbm, index_hbm, src_hbm, dst_hbm, count_hbm, basis_hbm, w1_hbm, w2_hbm, w3_hbm,
                 new_ref, out_ref,
                 f_ref, index_ref, src_ref, dst_ref, count_ref,
                 meta_ref, g_ref, bg_ref, mg_ref, w1_ref, w2_ref, w3_ref, table, w_mix,
                 part_ref, landed, edge_rows, fresh,
                 c_send, c_receive, t_send, t_receive, s_send, e_send, e_receive, local, p_send, p_receive,
                 n_send, n_receive):
    place = Place(sizes)
    z, nz = place.z, place.nz
    halo = index_ref.shape[1]
    na = out_ref.shape[0]
    atoms, width = g_ref.shape[1:]
    groups, slots = src_ref.shape
    radial = bg_ref.shape[2]
    lanes = -(-max(atoms, halo) // 128) * 128
    group = na * 3 * halo
    f32, bf16 = jnp.float32, jnp.bfloat16
    chunks = t_receive.shape[3]
    f_rows = atoms // chunks
    b_rows = halo // chunks
    edge_pairs = ((meta_ref, mg_ref), (basis_hbm, bg_ref))

    place.greet()
    inputs = [
        pltpu.make_async_copy(source, target, local.at[k])
        for k, (source, target) in enumerate(
            [(src_hbm, src_ref), (dst_hbm, dst_ref), (index_hbm, index_ref), (count_hbm, count_ref), (f_hbm, f_ref)]
        )
    ]
    weights = [
        pltpu.make_async_copy(source, target, local.at[5 + k])
        for k, (source, target) in enumerate(
            [(w1_hbm, w1_ref), (w2_hbm, w2_ref), (w3_hbm, w3_ref), (basis_hbm.at[z], bg_ref.at[z])]
        )
    ]
    for copy in inputs + weights:
        copy.start()
    rest = table.shape[0] - (nz + 2) * group
    table[(nz + 2) * group :, :] = jnp.zeros((rest, width), bf16)
    meta_ref[...] = jnp.zeros_like(meta_ref)
    for copy in inputs:
        copy.wait()
    edge_src = src_ref[...].astype(f32)
    beyond = edge_src - float(atoms)
    offset = jnp.floor((beyond + 0.5) * (1.0 / halo))
    slot = beyond - offset * float(halo)
    offset = jnp.where(offset >= 13.0, offset + 1.0, offset)
    off_x = jnp.floor((offset + 0.5) * (1.0 / 9.0))
    inner = offset - 9.0 * off_x
    off_y = jnp.floor((inner + 0.5) * (1.0 / 3.0))
    off_z = inner - 3.0 * off_y
    slot_x = jnp.where(off_x == 1.0, 0.0, jnp.where(off_x == 2.0, 1.0, float(na - 1)))
    position = float(atoms) + ((off_z * float(na) + slot_x) * 3.0 + off_y) * float(halo) + slot
    position = jnp.where(edge_src < float(atoms), edge_src, position)
    row_lane = lax.broadcasted_iota(jnp.int32, (1, slots), 1)
    index_row = index_ref[...].astype(f32)
    for j in range(groups):
        meta_ref[j, 0:1, :] = position[j : j + 1, :]
        target = jnp.where(row_lane < count_ref[j], dst_ref[j : j + 1, :], -1)
        meta_ref[j, 1:2, :] = target.astype(f32)
        meta_ref[j, 2:3, :halo] = index_row
    g_ref[z] = f_ref[...]
    mg_ref[z] = meta_ref[z]
    place.meet()

    def when(entry, action):
        s, sign = entry
        zz = z + sign * s
        if s == 0:
            action(zz)
        else:
            pl.when((zz >= 0) & (zz < nz))(functools.partial(action, zz))

    def feature(zz, k):
        return g_ref.at[zz, pl.ds(k * f_rows, f_rows)]

    def row_of(a, b, zz):
        return pl.multiple_of(((zz + 1) * (na * 3) + a * 3 + b) * halo, 16)

    def block(a, b, zz, k=None):
        if k is None:
            return table.at[pl.ds(row_of(a, b, zz), halo)]
        return table.at[pl.ds(pl.multiple_of(row_of(a, b, zz) + k * b_rows, 16), b_rows)]

    def arrival(a, b, zz, k=None):
        there = block(a, b, zz, k)
        k = 0 if k is None else k
        remote(there, there, t_send.at[0, 0, 0], t_receive.at[a, b, zz, k], place.first).wait_recv()

    def chain(entry, zz, k, do):
        s, sign = entry
        if s < nz - 1:
            for go in ((1, -1) if s == 0 else (-sign,)):
                device = (place.x, place.y, z + go)

                def act():
                    way = 0 if go > 0 else 1
                    do(remote(feature(zz, k), feature(zz, k), c_send.at[way, zz, k], c_receive.at[zz, k], device))

                pl.when((z + go >= 0) & (z + go < nz))(act)

    def to_siblings(b, zz, do):
        for i, device in enumerate(place.siblings):
            do(remote(block(0, b, zz), block(place.sibling_slot(i), b, zz), s_send.at[i, b, zz],
                      t_receive.at[place.sibling_slot(i), b, zz, 0], device))

    def pass_on(b, zz, k, do):
        own = isinstance(b, int)
        device, which = (place.first, 0) if own else (place.second, 1)
        do(remote(block(0, b, zz, k), block(0, place.b_second, zz, k), t_send.at[which, zz, k],
                  t_receive.at[0, place.b_second, zz, k], device))

    lane = lax.broadcasted_iota(jnp.int32, (lanes, lanes), 1).astype(f32)

    def boundary(index_row, rows):
        index = jnp.broadcast_to(index_row, (lanes, lanes)).T
        pick = (index == lane).astype(bf16)[:halo, :atoms]
        return jnp.dot(pick, rows, preferred_element_type=f32).astype(bf16)

    def own_stage(entry, do):
        s, sign = entry

        def act(zz):
            for k in range(chunks):
                if s > 0 and do is start:
                    remote(feature(zz, k), feature(zz, k), c_send.at[0, 0, 0], c_receive.at[zz, k], place.first).wait_recv()
                chain(entry, zz, k, do)
            if do is start:
                if s > 0:
                    edge(0, s if sign < 0 else nz - s, lambda copy: copy.wait_recv())
                table[pl.ds(row_of(0, 1, zz), halo), :] = boundary(mg_ref[zz, 2:3, :lanes], g_ref[zz])
            for k in range(chunks):
                pass_on(1, zz, k, do)
            to_siblings(1, zz, do)

        when(entry, act)

    def first_stage(entry, do):
        def act(zz):
            for k in range(chunks):
                if do is start:
                    arrival(0, place.b_first, zz, k)
                pass_on(place.b_first, zz, k, do)
            to_siblings(place.b_first, zz, do)

        when(entry, act)

    def second_stage(entry, do):
        def act(zz):
            if do is start:
                for k in range(chunks):
                    arrival(0, place.b_second, zz, k)
            to_siblings(place.b_second, zz, do)

        when(entry, act)

    def edge(q, step, do):
        own, grid = edge_pairs[q]
        device = place.along_z(step)
        do(remote(own.at[device[2]], grid.at[z], e_send.at[q, step], e_receive.at[q, step], device))

    def edges(q, do):
        for step in range(1, nz):
            edge(q, step, do)

    def start(copy):
        copy.start()

    def finish(copy):
        copy.wait_send()

    rounds = [[(0, 0)]] + [[(s, -1), (s, 1)] for s in range(1, nz)]
    for r in range(nz + 2):
        if r < nz:
            for entry in rounds[r]:
                own_stage(entry, start)
        if r == 0:
            edges(0, start)
        if r == nz - 1:
            edges(1, start)
        if 1 <= r <= nz:
            for entry in rounds[r - 1]:
                first_stage(entry, start)
        if r >= 2:
            for entry in rounds[r - 2]:
                second_stage(entry, start)
    for copy in weights:
        copy.wait()

    def project(o, carry):
        w_mix[o, :radial, :] = w1_ref[2 * width :, :]
        w_mix[o, radial:, :] = jnp.dot(
            g_ref[o], w1_ref[width : 2 * width, :], preferred_element_type=f32
        ).astype(bf16)
        return carry

    lax.fori_loop(0, nz, project, 0)
    for a in range(1, na):
        for step in range(nz):

            def last(zz, a=a):
                for b in (1, place.b_first, place.b_second):
                    arrival(a, b, zz)

            for entry in rounds[step]:
                when(entry, last)
    table[(nz + 1) * group : (nz + 2) * group, :] = table[group : 2 * group, :]
    table[:group, :] = table[nz * group : (nz + 1) * group, :]
    edges(1, lambda copy: copy.wait_recv())
    window = -(-3 * group // lanes) * lanes
    lane_s = lax.broadcasted_iota(jnp.int32, (slots, lanes), 1).astype(f32)
    sublane = lax.broadcasted_iota(jnp.int32, (atoms, slots), 0).astype(f32)

    def domain(o):
        position = jnp.broadcast_to(mg_ref[o, 0:1, :], (lanes, slots)).T
        target = jnp.broadcast_to(mg_ref[o, 1:2, :], (lanes, slots)).T
        own = g_ref[o]
        pick = (position == lane_s).astype(bf16)
        source = jnp.dot(pick, own, preferred_element_type=f32)
        picks = jnp.concatenate(
            [(position - float(atoms + j * lanes) == lane_s).astype(bf16) for j in range(window // lanes)],
            axis=1,
        )
        rows = table[pl.ds(pl.multiple_of(o * group, 16), window), :]
        source = source + jnp.dot(picks, rows, preferred_element_type=f32)
        mix = jnp.concatenate([bg_ref[o], (target == lane_s).astype(bf16)], axis=1)
        pre = jnp.dot(source.astype(bf16), w1_ref[:width, :], preferred_element_type=f32)
        pre = pre + jnp.dot(mix, w_mix[o], preferred_element_type=f32)
        half = 0.5 * pre
        hidden = (half + half * jnp.tanh(half)).astype(bf16)
        incidence = (jnp.broadcast_to(mg_ref[o, 1:2, :], (atoms, slots)) == sublane).astype(bf16)
        summed = jnp.dot(incidence, hidden, preferred_element_type=f32).astype(bf16)
        return jnp.dot(summed, w2_ref[...], preferred_element_type=f32)

    def returned(step):
        device = place.along_z(step + 1)
        return remote(part_ref.at[step], landed.at[step], p_send.at[step], p_receive.at[step], device)

    def other(step, carry):
        part_ref[step] = domain(lax.rem(z + step + 1, nz)).astype(bf16)
        returned(step).start()
        return carry

    lax.fori_loop(0, nz - 1, other, 0)
    total = domain(z)
    for step in range(nz - 1):
        returned(step).wait_recv()
        total = total + landed[step].astype(f32)
    mean_square = jnp.mean(total * total, axis=-1, keepdims=True)
    normed = (total * lax.rsqrt(mean_square + 1e-05)).astype(bf16)
    update = jnp.dot(normed, w3_ref[...], preferred_element_type=f32)
    new_rows = (f_ref[...].astype(f32) + update).astype(bf16)
    edge_rows[...] = boundary(meta_ref[0, 2:3, :lanes], new_rows)

    started = []

    def begin(b, c, k, kind, slot, device):
        index = 1 if b is None else b
        rows = pl.ds(0, halo) if k is None else pl.ds(k * b_rows, b_rows)
        if b is None and isinstance(c, int):
            source = edge_rows.at[rows]
        else:
            source = out_ref.at[0, index, c, rows]
        k = 0 if k is None else k
        copy = remote(source, out_ref.at[(*slot, rows)], n_send.at[kind, index, c, k], n_receive.at[(*slot, k)], device)
        copy.start()
        started.append(copy)

    def landing(a, b, c, k=None):
        rows = pl.ds(0, halo) if k is None else pl.ds(k * b_rows, b_rows)
        there = out_ref.at[a, b, c, rows]
        remote(there, there, n_send.at[0, 0, 0, 0], n_receive.at[a, b, c, 0 if k is None else k], place.first).wait_recv()

    def to_siblings_next(b, c):
        for i, device in enumerate(place.siblings):
            begin(b, c, None, 3 + i, (place.sibling_slot(i), 1 if b is None else b, c), device)

    for k in range(chunks):
        begin(None, 1, k, 0, (0, 1, 0), place.along_z(1))
        begin(None, 1, k, 1, (0, 1, 2), place.along_z(-1))
    for k in range(chunks):
        begin(None, 1, k, 2, (0, place.b_second, 1), place.first)
    to_siblings_next(None, 1)
    centre = pltpu.make_async_copy(edge_rows, out_ref.at[0, 1, 1], local.at[0])
    centre.start()
    fresh[...] = new_rows
    keep = pltpu.make_async_copy(fresh, new_ref, local.at[1])
    keep.start()
    near = jnp.where(z == 0, 2, 0)
    order = (1, near, 2 - near)

    def own_next(c):
        for k in range(chunks):
            landing(0, 1, c, k)
            begin(None, c, k, 2, (0, place.b_second, c), place.first)
        to_siblings_next(None, c)

    def first_next(c):
        for k in range(chunks):
            landing(0, place.b_first, c, k)
            begin(place.b_first, c, k, 2, (0, place.b_second, c), place.second)
        to_siblings_next(place.b_first, c)

    def second_next(c):
        for k in range(chunks):
            landing(0, place.b_second, c, k)
        to_siblings_next(place.b_second, c)

    own_next(order[1])
    first_next(order[0])
    own_next(order[2])
    first_next(order[1])
    second_next(order[0])
    first_next(order[2])
    second_next(order[1])
    second_next(order[2])
    for b in (1, place.b_first, place.b_second):
        for a in range(1, na):
            for c in order:
                landing(a, b, c)
    for group_ in rounds:
        for entry in group_:
            own_stage(entry, finish)
            first_stage(entry, finish)
            second_stage(entry, finish)
    for q in range(2):
        edges(q, finish)
    for step in range(nz - 1):
        returned(step).wait_send()
    for copy in started:
        copy.wait_send()
    keep.wait()
    centre.wait()


def spread_kernel(new_ref, blocks_ref, new_out, out_ref, row_sem, out_sem):
    na = blocks_ref.shape[0]
    parts = (1, 0, 1) if na == 2 else (2, 0, 1)
    stores = [pltpu.make_async_copy(new_ref, new_out, row_sem.at[0])]
    stores[0].start()
    for part, slot in enumerate(parts):
        for b in range(3):
            for c in range(3):
                cell = part * 9 + b * 3 + c
                if cell != 13:
                    cell = cell - 1 if cell > 13 else cell
                    stores.append(pltpu.make_async_copy(blocks_ref.at[slot, b, c], out_ref.at[cell], out_sem.at[cell]))
                    stores[-1].start()
    for copy in stores:
        copy.wait()


def shards(sizes, features, halo_index, edge_src, edge_dst, edge_count, edge_basis, w_edge_in, w_edge_out, w_update):
    nx, ny, nz = sizes
    atoms, width = features.shape
    groups, slots = edge_src.shape
    halo = halo_index.shape[0]
    radial = edge_basis.shape[1]
    hidden = w_edge_in.shape[2]
    lanes = -(-max(atoms, halo) // 128) * 128
    na = 2 if nx == 2 else 3
    f32, bf16 = jnp.float32, jnp.bfloat16
    basis = edge_basis.reshape(groups, slots, radial)
    anywhere = pl.BlockSpec(memory_space=pl.ANY)
    dma = pltpu.SemaphoreType.DMA
    chunks = 2
    hbm = functools.partial(pltpu.with_memory_space_constraint, memory_space=pltpu.HBM)
    group = na * 3 * halo
    window = -(-3 * group // lanes) * lanes
    table_rows = (nz - 1) * group + window
    new_rows, blocks = pl.pallas_call(
        functools.partial(layer_kernel, sizes),
        out_shape=(
            pltpu.VMEM((atoms, width), bf16),
            pltpu.VMEM((na, 3, 3, halo, width), bf16),
        ),
        in_specs=[anywhere] * 9,
        out_specs=(anywhere, anywhere),
        scratch_shapes=[
            pltpu.VMEM((atoms, width), bf16),
            pltpu.VMEM((1, halo), jnp.int32),
            pltpu.VMEM((groups, slots), jnp.int32),
            pltpu.VMEM((groups, slots), jnp.int32),
            pltpu.SMEM((groups,), jnp.int32),
            pltpu.VMEM((nz, 8, slots), f32),
            pltpu.VMEM((nz, atoms, width), bf16),
            pltpu.VMEM((nz, slots, radial), bf16),
            pltpu.VMEM((nz, 8, slots), f32),
            pltpu.VMEM(w_edge_in.shape[1:], bf16),
            pltpu.VMEM(w_edge_out.shape[1:], bf16),
            pltpu.VMEM(w_update.shape, bf16),
            pltpu.VMEM((table_rows, width), bf16),
            pltpu.VMEM((nz, radial + lanes, hidden), bf16),
            pltpu.VMEM((nz - 1, atoms, width), bf16),
            pltpu.VMEM((nz - 1, atoms, width), bf16),
            pltpu.VMEM((halo, width), bf16),
            pltpu.VMEM((atoms, width), bf16),
            dma((2, nz, chunks)),
            dma((nz, chunks)),
            dma((2, nz, chunks)),
            dma((na, 3, nz, chunks)),
            dma((na - 1, 3, nz)),
            dma((2, nz)),
            dma((2, nz)),
            dma((9,)),
            dma((nz - 1,)),
            dma((nz - 1,)),
            dma((3 + na - 1, 3, 3, chunks)),
            dma((na, 3, 3, chunks)),
        ],
        compiler_params=pltpu.CompilerParams(
            collective_id=0, has_side_effects=True, vmem_limit_bytes=56 * 1024 * 1024
        ),
        name="layer",
    )(*(hbm(array) for array in (features, halo_index.reshape(1, halo), edge_src, edge_dst, edge_count, basis,
                                  w_edge_in[0], w_edge_out[0], w_update)))
    blocks = pltpu.with_memory_space_constraint(blocks, pltpu.VMEM)
    new_rows = pltpu.with_memory_space_constraint(new_rows, pltpu.VMEM)
    return pl.pallas_call(
        spread_kernel,
        out_shape=(
            jax.ShapeDtypeStruct((atoms, width), bf16),
            jax.ShapeDtypeStruct((26, halo, width), bf16),
        ),
        in_specs=[anywhere, anywhere],
        out_specs=(anywhere, anywhere),
        scratch_shapes=[
            dma((1,)),
            dma((26,)),
        ],
        name="spread",
    )(new_rows, blocks)


def solution(mesh):
    sizes = tuple(mesh.shape[name] for name in AXES)
    in_specs = (
        P(AXES, None),
        P(AXES),
        P(AXES, None),
        P(AXES, None),
        P(AXES),
        P(AXES, None),
        P("gz", None, None),
        P("gz", None, None),
        P(),
    )
    out_specs = (P(AXES, None), P(AXES, None, None))
    return jax.shard_map(
        functools.partial(shards, sizes), mesh=mesh, in_specs=in_specs, out_specs=out_specs, check_vma=False
    )
```

```python
import functools

import jax
import jax.numpy as jnp
from jax import lax
from jax.experimental import pallas as pl
from jax.experimental.pallas import tpu as pltpu
from jax.sharding import PartitionSpec as P

AXES = ("gx", "gy", "gz")
MESH = pl.DeviceIdType.MESH


class Place:
    def __init__(self, sizes):
        self.nx, self.ny, self.nz = sizes
        self.x, self.y, self.z = (lax.axis_index(name) for name in AXES)
        x, y, z = self.x, self.y, self.z
        self.first = (x, y + 1 - 2 * lax.rem(y, 2), z)
        self.second = (x, lax.rem(y + 2, 4), z)
        self.diagonal = (x, lax.rem(y + 3 - 2 * lax.rem(y, 2), 4), z)
        self.b_first = 2 - 2 * lax.rem(y, 2)
        self.b_second = 2 * lax.rem(y, 2)
        self.siblings = [(lax.rem(x + 1, self.nx), y, z)]
        if self.nx > 2:
            self.siblings.append((lax.rem(x + self.nx - 1, self.nx), y, z))

    def along_z(self, step):
        return (self.x, self.y, lax.rem(self.z + step + self.nz, self.nz))

    def sibling_slot(self, index):
        return 1 if self.nx == 2 else 2 - index

    def greet(self):
        self.barrier = pltpu.get_barrier_semaphore()
        partners = [self.along_z(step) for step in range(1, self.nz)]
        partners += [self.first, self.second, self.diagonal] + self.siblings
        for partner in partners:
            pl.semaphore_signal(self.barrier, inc=1, device_id=partner, device_id_type=MESH)
        self.partners = len(partners)

    def meet(self):
        pl.semaphore_wait(self.barrier, self.partners)


def remote(source, target, send, receive, device):
    return pltpu.make_async_remote_copy(
        src_ref=source,
        dst_ref=target,
        send_sem=send,
        recv_sem=receive,
        device_id=device,
        device_id_type=MESH,
    )


def layer_kernel(sizes, f_hbm, index_hbm, src_hbm, dst_hbm, count_hbm, basis_hbm, w1_hbm, w2_hbm, w3_hbm,
                 new_ref, out_ref,
                 f_ref, index_ref, src_ref, dst_ref, count_ref,
                 meta_ref, g_ref, bg_ref, mg_ref, w1_ref, w2_ref, w3_ref, table, w_mix,
                 part_ref, landed, edge_rows, fresh,
                 c_send, c_receive, t_send, t_receive, s_send, e_send, e_receive, local, p_send, p_receive,
                 n_send, n_receive):
    place = Place(sizes)
    z, nz = place.z, place.nz
    halo = index_ref.shape[1]
    na = out_ref.shape[0]
    atoms, width = g_ref.shape[1:]
    groups, slots = src_ref.shape
    radial = bg_ref.shape[2]
    lanes = -(-max(atoms, halo) // 128) * 128
    group = na * 3 * halo
    f32, bf16 = jnp.float32, jnp.bfloat16
    chunks = t_receive.shape[3]
    pieces = c_receive.shape[1]
    f_rows = atoms // pieces
    b_rows = halo // chunks
    chunks_next = n_receive.shape[3]
    n_rows = halo // chunks_next
    edge_pairs = ((meta_ref, mg_ref), (basis_hbm, bg_ref))

    place.greet()
    inputs = [
        pltpu.make_async_copy(source, target, local.at[k])
        for k, (source, target) in enumerate(
            [(src_hbm, src_ref), (dst_hbm, dst_ref), (index_hbm, index_ref), (count_hbm, count_ref), (f_hbm, f_ref)]
        )
    ]
    weights = [
        pltpu.make_async_copy(source, target, local.at[5 + k])
        for k, (source, target) in enumerate(
            [(w1_hbm, w1_ref), (w2_hbm, w2_ref), (w3_hbm, w3_ref), (basis_hbm.at[z], bg_ref.at[z])]
        )
    ]
    for copy in inputs + weights:
        copy.start()
    rest = table.shape[0] - (nz + 2) * group
    table[(nz + 2) * group :, :] = jnp.zeros((rest, width), bf16)
    meta_ref[...] = jnp.zeros_like(meta_ref)
    for copy in inputs:
        copy.wait()
    edge_src = src_ref[...].astype(f32)
    beyond = edge_src - float(atoms)
    offset = jnp.floor((beyond + 0.5) * (1.0 / halo))
    slot = beyond - offset * float(halo)
    offset = jnp.where(offset >= 13.0, offset + 1.0, offset)
    off_x = jnp.floor((offset + 0.5) * (1.0 / 9.0))
    inner = offset - 9.0 * off_x
    off_y = jnp.floor((inner + 0.5) * (1.0 / 3.0))
    off_z = inner - 3.0 * off_y
    slot_x = jnp.where(off_x == 1.0, 0.0, jnp.where(off_x == 2.0, 1.0, float(na - 1)))
    position = float(atoms) + ((off_z * float(na) + slot_x) * 3.0 + off_y) * float(halo) + slot
    position = jnp.where(edge_src < float(atoms), edge_src, position)
    row_lane = lax.broadcasted_iota(jnp.int32, (1, slots), 1)
    index_row = index_ref[...].astype(f32)
    for j in range(groups):
        meta_ref[j, 0:1, :] = position[j : j + 1, :]
        target = jnp.where(row_lane < count_ref[j], dst_ref[j : j + 1, :], -1)
        meta_ref[j, 1:2, :] = target.astype(f32)
        meta_ref[j, 2:3, :halo] = index_row
    g_ref[z] = f_ref[...]
    mg_ref[z] = meta_ref[z]

    def when(entry, action):
        s, sign = entry
        zz = z + sign * s
        if s == 0:
            action(zz)
        else:
            pl.when((zz >= 0) & (zz < nz))(functools.partial(action, zz))

    def feature(zz, k):
        return g_ref.at[zz, pl.ds(k * f_rows, f_rows)]

    def row_of(a, b, zz):
        return pl.multiple_of(((zz + 1) * (na * 3) + a * 3 + b) * halo, 16)

    def block(a, b, zz, k=None):
        if k is None:
            return table.at[pl.ds(row_of(a, b, zz), halo)]
        return table.at[pl.ds(pl.multiple_of(row_of(a, b, zz) + k * b_rows, 16), b_rows)]

    def arrival(a, b, zz, k=None):
        there = block(a, b, zz, k)
        k = 0 if k is None else k
        remote(there, there, t_send.at[0, 0, 0], t_receive.at[a, b, zz, k], place.first).wait_recv()

    def chain(entry, zz, k, do):
        s, sign = entry
        if s < nz - 1:
            for go in ((1, -1) if s == 0 else (-sign,)):
                device = (place.x, place.y, z + go)

                def act():
                    way = 0 if go > 0 else 1
                    do(remote(feature(zz, k), feature(zz, k), c_send.at[way, zz, k], c_receive.at[zz, k], device))

                pl.when((z + go >= 0) & (z + go < nz))(act)

    def to_siblings(b, zz, do):
        for i, device in enumerate(place.siblings):
            do(remote(block(0, b, zz), block(place.sibling_slot(i), b, zz), s_send.at[i, b, zz],
                      t_receive.at[place.sibling_slot(i), b, zz, 0], device))

    def pass_on(b, zz, k, which, do):
        device = (place.first, place.second, place.diagonal)[which]
        slot = place.b_first if which == 2 else place.b_second
        do(remote(block(0, b, zz, k), block(0, slot, zz, k), t_send.at[which, zz, k],
                  t_receive.at[0, slot, zz, k], device))

    lane = lax.broadcasted_iota(jnp.int32, (lanes, lanes), 1).astype(f32)

    def boundary(index_row, rows):
        index = jnp.broadcast_to(index_row, (lanes, lanes)).T
        pick = (index == lane).astype(bf16)[:halo, :atoms]
        return jnp.dot(pick, rows, preferred_element_type=f32).astype(bf16)

    table[pl.ds(row_of(0, 1, z), halo), :] = boundary(meta_ref[0, 2:3, :lanes], f_ref[...])
    place.meet()

    def own_stage(entry, do):
        s, sign = entry

        def act(zz):
            for k in range(pieces):
                if s > 0 and do is start:
                    remote(feature(zz, k), feature(zz, k), c_send.at[0, 0, 0], c_receive.at[zz, k], place.first).wait_recv()
                chain(entry, zz, k, do)
            if s > 0 and do is start:
                edge(0, s if sign < 0 else nz - s, lambda copy: copy.wait_recv())
                table[pl.ds(row_of(0, 1, zz), halo), :] = boundary(mg_ref[zz, 2:3, :lanes], g_ref[zz])
            for k in range(chunks):
                pass_on(1, zz, k, 0, do)
                if s in straight:
                    pass_on(1, zz, k, 2, do)
            to_siblings(1, zz, do)

        when(entry, act)

    def first_stage(entry, do):
        def act(zz):
            for k in range(chunks):
                if do is start:
                    arrival(0, place.b_first, zz, k)
                if entry[0] not in straight:
                    pass_on(place.b_first, zz, k, 1, do)
            to_siblings(place.b_first, zz, do)

        when(entry, act)

    def second_stage(entry, do):
        def act(zz):
            if do is start:
                for k in range(chunks):
                    arrival(0, place.b_second, zz, k)
            to_siblings(place.b_second, zz, do)

        when(entry, act)

    def edge(q, step, do):
        own, grid = edge_pairs[q]
        device = place.along_z(step)
        do(remote(own.at[device[2]], grid.at[z], e_send.at[q, step], e_receive.at[q, step], device))

    def edges(q, do):
        for step in range(1, nz):
            edge(q, step, do)

    def start(copy):
        copy.start()

    def finish(copy):
        copy.wait_send()

    straight = ()
    rounds = [[(0, 0)]] + [[(s, -1), (s, 1)] for s in range(1, nz)]
    for r in range(nz + 2):
        if r < nz:
            for entry in rounds[r]:
                own_stage(entry, start)
        if r == 0:
            edges(0, start)
        if r == nz:
            edges(1, start)
        if 1 <= r <= nz:
            for entry in rounds[r - 1]:
                first_stage(entry, start)
        if r >= 2:
            for entry in rounds[r - 2]:
                second_stage(entry, start)
    for copy in weights:
        copy.wait()

    def project(o, carry):
        w_mix[o, :radial, :] = w1_ref[2 * width :, :]
        w_mix[o, radial:, :] = jnp.dot(
            g_ref[o], w1_ref[width : 2 * width, :], preferred_element_type=f32
        ).astype(bf16)
        return carry

    lax.fori_loop(0, nz, project, 0)
    for a in range(1, na):
        for step in range(nz):

            def last(zz, a=a):
                for b in (1, place.b_first, place.b_second):
                    arrival(a, b, zz)

            for entry in rounds[step]:
                when(entry, last)
    table[(nz + 1) * group : (nz + 2) * group, :] = table[group : 2 * group, :]
    table[:group, :] = table[nz * group : (nz + 1) * group, :]
    edges(1, lambda copy: copy.wait_recv())
    window = -(-3 * group // lanes) * lanes
    lane_s = lax.broadcasted_iota(jnp.int32, (slots, lanes), 1).astype(f32)
    sublane = lax.broadcasted_iota(jnp.int32, (atoms, slots), 0).astype(f32)

    def domain(o):
        position = jnp.broadcast_to(mg_ref[o, 0:1, :], (lanes, slots)).T
        target = jnp.broadcast_to(mg_ref[o, 1:2, :], (lanes, slots)).T
        own = g_ref[o]
        pick = (position == lane_s).astype(bf16)
        source = jnp.dot(pick, own, preferred_element_type=f32)
        picks = jnp.concatenate(
            [(position - float(atoms + j * lanes) == lane_s).astype(bf16) for j in range(window // lanes)],
            axis=1,
        )
        rows = table[pl.ds(pl.multiple_of(o * group, 16), window), :]
        source = source + jnp.dot(picks, rows, preferred_element_type=f32)
        mix = jnp.concatenate([bg_ref[o], (target == lane_s).astype(bf16)], axis=1)
        pre = jnp.dot(source.astype(bf16), w1_ref[:width, :], preferred_element_type=f32)
        pre = pre + jnp.dot(mix, w_mix[o], preferred_element_type=f32)
        half = 0.5 * pre
        hidden = (half + half * jnp.tanh(half)).astype(bf16)
        incidence = (jnp.broadcast_to(mg_ref[o, 1:2, :], (atoms, slots)) == sublane).astype(bf16)
        summed = jnp.dot(incidence, hidden, preferred_element_type=f32).astype(bf16)
        return jnp.dot(summed, w2_ref[...], preferred_element_type=f32)

    def returned(step):
        device = place.along_z(step + 1)
        return remote(part_ref.at[step], landed.at[step], p_send.at[step], p_receive.at[step], device)

    def other(step, carry):
        part_ref[step] = domain(lax.rem(z + step + 1, nz)).astype(bf16)
        returned(step).start()
        return carry

    lax.fori_loop(0, nz - 1, other, 0)
    total = domain(z)
    for step in range(nz - 1):
        returned(step).wait_recv()
        total = total + landed[step].astype(f32)
    mean_square = jnp.mean(total * total, axis=-1, keepdims=True)
    normed = (total * lax.rsqrt(mean_square + 1e-05)).astype(bf16)
    update = jnp.dot(normed, w3_ref[...], preferred_element_type=f32)
    new_rows = (f_ref[...].astype(f32) + update).astype(bf16)
    edge_rows[...] = boundary(meta_ref[0, 2:3, :lanes], new_rows)

    started = []

    def begin(b, c, k, kind, slot, device):
        index = 1 if b is None else b
        rows = pl.ds(0, halo) if k is None else pl.ds(k * n_rows, n_rows)
        if b is None and isinstance(c, int):
            source = edge_rows.at[rows]
        else:
            source = out_ref.at[0, index, c, rows]
        k = 0 if k is None else k
        copy = remote(source, out_ref.at[(*slot, rows)], n_send.at[kind, index, c, k], n_receive.at[(*slot, k)], device)
        copy.start()
        started.append(copy)

    def landing(a, b, c, k=None):
        rows = pl.ds(0, halo) if k is None else pl.ds(k * n_rows, n_rows)
        there = out_ref.at[a, b, c, rows]
        remote(there, there, n_send.at[0, 0, 0, 0], n_receive.at[a, b, c, 0 if k is None else k], place.first).wait_recv()

    def to_siblings_next(b, c):
        for i, device in enumerate(place.siblings):
            begin(b, c, None, 4 + i, (place.sibling_slot(i), 1 if b is None else b, c), device)

    for k in range(chunks_next):
        begin(None, 1, k, 0, (0, 1, 0), place.along_z(1))
        begin(None, 1, k, 1, (0, 1, 2), place.along_z(-1))
    for k in range(chunks_next):
        begin(None, 1, k, 3, (0, place.b_first, 1), place.diagonal)
    for k in range(chunks_next):
        begin(None, 1, k, 2, (0, place.b_second, 1), place.first)
    to_siblings_next(None, 1)
    centre = pltpu.make_async_copy(edge_rows, out_ref.at[0, 1, 1], local.at[0])
    centre.start()
    fresh[...] = new_rows
    keep = pltpu.make_async_copy(fresh, new_ref, local.at[1])
    keep.start()
    near = jnp.where(z == 0, 2, 0)
    order = (1, near, 2 - near)

    def own_next(c):
        for k in range(chunks_next):
            landing(0, 1, c, k)
            begin(None, c, k, 2, (0, place.b_second, c), place.first)
        to_siblings_next(None, c)

    def other_next(b, c):
        for k in range(chunks_next):
            landing(0, b, c, k)
            if b is place.b_second and isinstance(c, int):
                begin(b, c, k, 0, (0, b, 0), place.along_z(1))
                begin(b, c, k, 1, (0, b, 2), place.along_z(-1))
        to_siblings_next(b, c)

    own_next(order[1])
    other_next(place.b_second, 1)
    own_next(order[2])
    for c in order:
        other_next(place.b_first, c)
    for c in order[1:]:
        other_next(place.b_second, c)
    for b in (1, place.b_first, place.b_second):
        for a in range(1, na):
            for c in order:
                landing(a, b, c)
    for group_ in rounds:
        for entry in group_:
            own_stage(entry, finish)
            first_stage(entry, finish)
            second_stage(entry, finish)
    for q in range(2):
        edges(q, finish)
    for step in range(nz - 1):
        returned(step).wait_send()
    for copy in started:
        copy.wait_send()
    keep.wait()
    centre.wait()


def spread_kernel(new_ref, blocks_ref, new_out, out_ref, row_sem, out_sem):
    na = blocks_ref.shape[0]
    parts = (1, 0, 1) if na == 2 else (2, 0, 1)
    stores = [pltpu.make_async_copy(new_ref, new_out, row_sem.at[0])]
    stores[0].start()
    for part, slot in enumerate(parts):
        for b in range(3):
            for c in range(3):
                cell = part * 9 + b * 3 + c
                if cell != 13:
                    cell = cell - 1 if cell > 13 else cell
                    stores.append(pltpu.make_async_copy(blocks_ref.at[slot, b, c], out_ref.at[cell], out_sem.at[cell]))
                    stores[-1].start()
    for copy in stores:
        copy.wait()


def shards(sizes, features, halo_index, edge_src, edge_dst, edge_count, edge_basis, w_edge_in, w_edge_out, w_update):
    nx, ny, nz = sizes
    atoms, width = features.shape
    groups, slots = edge_src.shape
    halo = halo_index.shape[0]
    radial = edge_basis.shape[1]
    hidden = w_edge_in.shape[2]
    lanes = -(-max(atoms, halo) // 128) * 128
    na = 2 if nx == 2 else 3
    f32, bf16 = jnp.float32, jnp.bfloat16
    basis = edge_basis.reshape(groups, slots, radial)
    anywhere = pl.BlockSpec(memory_space=pl.ANY)
    dma = pltpu.SemaphoreType.DMA
    chunks = 1
    pieces = 1
    chunks_next = 1
    hbm = functools.partial(pltpu.with_memory_space_constraint, memory_space=pltpu.HBM)
    group = na * 3 * halo
    window = -(-3 * group // lanes) * lanes
    table_rows = (nz - 1) * group + window
    new_rows, blocks = pl.pallas_call(
        functools.partial(layer_kernel, sizes),
        out_shape=(
            pltpu.VMEM((atoms, width), bf16),
            pltpu.VMEM((na, 3, 3, halo, width), bf16),
        ),
        in_specs=[anywhere] * 9,
        out_specs=(anywhere, anywhere),
        scratch_shapes=[
            pltpu.VMEM((atoms, width), bf16),
            pltpu.VMEM((1, halo), jnp.int32),
            pltpu.VMEM((groups, slots), jnp.int32),
            pltpu.VMEM((groups, slots), jnp.int32),
            pltpu.SMEM((groups,), jnp.int32),
            pltpu.VMEM((nz, 8, slots), f32),
            pltpu.VMEM((nz, atoms, width), bf16),
            pltpu.VMEM((nz, slots, radial), bf16),
            pltpu.VMEM((nz, 8, slots), f32),
            pltpu.VMEM(w_edge_in.shape[1:], bf16),
            pltpu.VMEM(w_edge_out.shape[1:], bf16),
            pltpu.VMEM(w_update.shape, bf16),
            pltpu.VMEM((table_rows, width), bf16),
            pltpu.VMEM((nz, radial + lanes, hidden), bf16),
            pltpu.VMEM((nz - 1, atoms, width), bf16),
            pltpu.VMEM((nz - 1, atoms, width), bf16),
            pltpu.VMEM((halo, width), bf16),
            pltpu.VMEM((atoms, width), bf16),
            dma((2, nz, pieces)),
            dma((nz, pieces)),
            dma((3, nz, chunks)),
            dma((na, 3, nz, chunks)),
            dma((na - 1, 3, nz)),
            dma((2, nz)),
            dma((2, nz)),
            dma((9,)),
            dma((nz - 1,)),
            dma((nz - 1,)),
            dma((4 + na - 1, 3, 3, chunks_next)),
            dma((na, 3, 3, chunks_next)),
        ],
        compiler_params=pltpu.CompilerParams(
            collective_id=0, has_side_effects=True, vmem_limit_bytes=56 * 1024 * 1024
        ),
        name="layer",
    )(*(hbm(array) for array in (features, halo_index.reshape(1, halo), edge_src, edge_dst, edge_count, basis,
                                  w_edge_in[0], w_edge_out[0], w_update)))
    blocks = pltpu.with_memory_space_constraint(blocks, pltpu.VMEM)
    new_rows = pltpu.with_memory_space_constraint(new_rows, pltpu.VMEM)
    return pl.pallas_call(
        spread_kernel,
        out_shape=(
            jax.ShapeDtypeStruct((atoms, width), bf16),
            jax.ShapeDtypeStruct((26, halo, width), bf16),
        ),
        in_specs=[anywhere, anywhere],
        out_specs=(anywhere, anywhere),
        scratch_shapes=[
            dma((1,)),
            dma((26,)),
        ],
        name="spread",
    )(new_rows, blocks)


def solution(mesh):
    sizes = tuple(mesh.shape[name] for name in AXES)
    in_specs = (
        P(AXES, None),
        P(AXES),
        P(AXES, None),
        P(AXES, None),
        P(AXES),
        P(AXES, None),
        P("gz", None, None),
        P("gz", None, None),
        P(),
    )
    out_specs = (P(AXES, None), P(AXES, None, None))
    return jax.shard_map(
        functools.partial(shards, sizes), mesh=mesh, in_specs=in_specs, out_specs=out_specs, check_vma=False
    )
```

```python
import functools

import jax
import jax.numpy as jnp
from jax import lax
from jax.experimental import pallas as pl
from jax.experimental.pallas import tpu as pltpu
from jax.sharding import PartitionSpec as P

AXES = ("gx", "gy", "gz")
MESH = pl.DeviceIdType.MESH


class Place:
    def __init__(self, sizes):
        self.nx, self.ny, self.nz = sizes
        self.x, self.y, self.z = (lax.axis_index(name) for name in AXES)
        x, y, z = self.x, self.y, self.z
        self.first = (x, y + 1 - 2 * lax.rem(y, 2), z)
        self.second = (x, lax.rem(y + 2, 4), z)
        self.diagonal = (x, lax.rem(y + 3 - 2 * lax.rem(y, 2), 4), z)
        self.b_first = 2 - 2 * lax.rem(y, 2)
        self.b_second = 2 * lax.rem(y, 2)
        self.siblings = [(lax.rem(x + 1, self.nx), y, z)]
        if self.nx > 2:
            self.siblings.append((lax.rem(x + self.nx - 1, self.nx), y, z))

    def along_z(self, step):
        return (self.x, self.y, lax.rem(self.z + step + self.nz, self.nz))

    def sibling_slot(self, index):
        return 1 if self.nx == 2 else 2 - index

    def greet(self):
        self.barrier = pltpu.get_barrier_semaphore()
        partners = [self.along_z(step) for step in range(1, self.nz)]
        partners += [self.first, self.second, self.diagonal] + self.siblings
        for partner in partners:
            pl.semaphore_signal(self.barrier, inc=1, device_id=partner, device_id_type=MESH)
        self.partners = len(partners)

    def meet(self):
        pl.semaphore_wait(self.barrier, self.partners)


def remote(source, target, send, receive, device):
    return pltpu.make_async_remote_copy(
        src_ref=source,
        dst_ref=target,
        send_sem=send,
        recv_sem=receive,
        device_id=device,
        device_id_type=MESH,
    )


def layer_kernel(sizes, f_hbm, index_hbm, src_hbm, dst_hbm, count_hbm, basis_hbm, w1_hbm, w2_hbm, w3_hbm,
                 new_ref, out_ref,
                 f_ref, index_ref, src_ref, dst_ref, count_ref,
                 meta_ref, g_ref, bg_ref, mg_ref, w1_ref, w2_ref, w3_ref, table, w_mix,
                 part_ref, landed, edge_rows, fresh,
                 c_send, c_receive, t_send, t_receive, s_send, e_send, e_receive, local, p_send, p_receive,
                 n_send, n_receive):
    place = Place(sizes)
    z, nz = place.z, place.nz
    halo = index_ref.shape[1]
    na = out_ref.shape[0]
    atoms, width = g_ref.shape[1:]
    groups, slots = src_ref.shape
    radial = bg_ref.shape[2]
    lanes = meta_ref.shape[2]
    parts = slots // lanes
    group = na * 3 * halo
    f32, bf16 = jnp.float32, jnp.bfloat16
    chunks = t_receive.shape[3]
    pieces = c_receive.shape[1]
    f_rows = atoms // pieces
    b_rows = halo // chunks
    chunks_next = n_receive.shape[3]
    n_rows = halo // chunks_next
    edge_pairs = ((meta_ref, mg_ref), (basis_hbm, bg_ref))

    place.greet()
    inputs = [
        pltpu.make_async_copy(source, target, local.at[k])
        for k, (source, target) in enumerate(
            [(src_hbm, src_ref), (dst_hbm, dst_ref), (index_hbm, index_ref), (count_hbm, count_ref), (f_hbm, f_ref)]
        )
    ]
    weights = [
        pltpu.make_async_copy(source, target, local.at[5 + k])
        for k, (source, target) in enumerate(
            [(w1_hbm, w1_ref), (w2_hbm, w2_ref), (w3_hbm, w3_ref), (basis_hbm.at[z], bg_ref.at[z])]
        )
    ]
    for copy in inputs + weights:
        copy.start()
    rest = table.shape[0] - (nz + 2) * group
    table[(nz + 2) * group :, :] = jnp.zeros((rest, width), bf16)
    meta_ref[...] = jnp.zeros_like(meta_ref)
    for copy in inputs:
        copy.wait()
    edge_src = src_ref[...].astype(f32)
    beyond = edge_src - float(atoms)
    offset = jnp.floor((beyond + 0.5) * (1.0 / halo))
    slot = beyond - offset * float(halo)
    offset = jnp.where(offset >= 13.0, offset + 1.0, offset)
    off_x = jnp.floor((offset + 0.5) * (1.0 / 9.0))
    inner = offset - 9.0 * off_x
    off_y = jnp.floor((inner + 0.5) * (1.0 / 3.0))
    off_z = inner - 3.0 * off_y
    slot_x = jnp.where(off_x == 1.0, 0.0, jnp.where(off_x == 2.0, 1.0, float(na - 1)))
    position = float(atoms) + ((off_z * float(na) + slot_x) * 3.0 + off_y) * float(halo) + slot
    position = jnp.where(edge_src < float(atoms), edge_src, position)
    row_lane = lax.broadcasted_iota(jnp.int32, (1, slots), 1)
    index_row = index_ref[...].astype(f32)
    for j in range(groups):
        target = jnp.where(row_lane < count_ref[j], dst_ref[j : j + 1, :], -1).astype(f32)
        for q in range(parts):
            meta_ref[j, q : q + 1, :] = position[j : j + 1, q * lanes : (q + 1) * lanes]
            meta_ref[j, parts + q : parts + q + 1, :] = target[:, q * lanes : (q + 1) * lanes]
        meta_ref[j, 2 * parts : 2 * parts + 1, :halo] = index_row
    g_ref[z] = f_ref[...]
    mg_ref[z] = meta_ref[z]

    def when(entry, action):
        s, sign = entry
        zz = z + sign * s
        if s == 0:
            action(zz)
        else:
            pl.when((zz >= 0) & (zz < nz))(functools.partial(action, zz))

    def feature(zz, k):
        return g_ref.at[zz, pl.ds(k * f_rows, f_rows)]

    def row_of(a, b, zz):
        return pl.multiple_of(((zz + 1) * (na * 3) + a * 3 + b) * halo, 16)

    def block(a, b, zz, k=None):
        if k is None:
            return table.at[pl.ds(row_of(a, b, zz), halo)]
        return table.at[pl.ds(pl.multiple_of(row_of(a, b, zz) + k * b_rows, 16), b_rows)]

    def arrival(a, b, zz, k=None):
        there = block(a, b, zz, k)
        k = 0 if k is None else k
        remote(there, there, t_send.at[0, 0, 0], t_receive.at[a, b, zz, k], place.first).wait_recv()

    def chain(entry, zz, k, do):
        s, sign = entry
        if s < nz - 1:
            for go in ((1, -1) if s == 0 else (-sign,)):
                device = (place.x, place.y, z + go)

                def act():
                    way = 0 if go > 0 else 1
                    do(remote(feature(zz, k), feature(zz, k), c_send.at[way, zz, k], c_receive.at[zz, k], device))

                pl.when((z + go >= 0) & (z + go < nz))(act)

    def to_siblings(b, zz, do):
        for i, device in enumerate(place.siblings):
            do(remote(block(0, b, zz), block(place.sibling_slot(i), b, zz), s_send.at[i, b, zz],
                      t_receive.at[place.sibling_slot(i), b, zz, 0], device))

    def pass_on(b, zz, k, which, do):
        device = (place.first, place.second, place.diagonal)[which]
        slot = place.b_first if which == 2 else place.b_second
        do(remote(block(0, b, zz, k), block(0, slot, zz, k), t_send.at[which, zz, k],
                  t_receive.at[0, slot, zz, k], device))

    lane = lax.broadcasted_iota(jnp.int32, (lanes, lanes), 1).astype(f32)

    def boundary(index_row, rows):
        index = jnp.broadcast_to(index_row, (lanes, lanes)).T
        pick = (index == lane).astype(bf16)[:halo, :atoms]
        return jnp.dot(pick, rows, preferred_element_type=f32).astype(bf16)

    table[pl.ds(row_of(0, 1, z), halo), :] = boundary(meta_ref[0, 2 * parts : 2 * parts + 1, :], f_ref[...])
    place.meet()

    def own_stage(entry, do):
        s, sign = entry

        def act(zz):
            for k in range(pieces):
                if s > 0 and do is start:
                    remote(feature(zz, k), feature(zz, k), c_send.at[0, 0, 0], c_receive.at[zz, k], place.first).wait_recv()
                chain(entry, zz, k, do)
            if s > 0 and do is start:
                edge(0, s if sign < 0 else nz - s, lambda copy: copy.wait_recv())
                table[pl.ds(row_of(0, 1, zz), halo), :] = boundary(mg_ref[zz, 2 * parts : 2 * parts + 1, :], g_ref[zz])
            for k in range(chunks):
                pass_on(1, zz, k, 0, do)
                if s in straight:
                    pass_on(1, zz, k, 2, do)
            to_siblings(1, zz, do)

        when(entry, act)

    def first_stage(entry, do):
        def act(zz):
            for k in range(chunks):
                if do is start:
                    arrival(0, place.b_first, zz, k)
                if entry[0] not in straight:
                    pass_on(place.b_first, zz, k, 1, do)
            to_siblings(place.b_first, zz, do)

        when(entry, act)

    def second_stage(entry, do):
        def act(zz):
            if do is start:
                for k in range(chunks):
                    arrival(0, place.b_second, zz, k)
            to_siblings(place.b_second, zz, do)

        when(entry, act)

    def edge(q, step, do):
        own, grid = edge_pairs[q]
        device = place.along_z(step)
        do(remote(own.at[device[2]], grid.at[z], e_send.at[q, step], e_receive.at[q, step], device))

    def edges(q, do):
        for step in range(1, nz):
            edge(q, step, do)

    def basis(ends):
        for step in range(1, nz):
            goal = lax.rem(z + step, nz)
            last = (goal == 0) | (goal == nz - 1)
            pl.when(last if ends else jnp.logical_not(last))(functools.partial(edge, 1, step, start))

    def start(copy):
        copy.start()

    def finish(copy):
        copy.wait_send()

    straight = ()
    rounds = [[(0, 0)]] + [[(s, -1), (s, 1)] for s in range(1, nz)]
    for r in range(nz + 2):
        if r < nz:
            for entry in rounds[r]:
                own_stage(entry, start)
        if r == 0:
            edges(0, start)
        if r == 3:
            basis(False)
        if r == nz:
            basis(True)
        if 1 <= r <= nz:
            for entry in rounds[r - 1]:
                first_stage(entry, start)
        if r >= 2:
            for entry in rounds[r - 2]:
                second_stage(entry, start)
    for copy in weights:
        copy.wait()

    def project(o, carry):
        w_mix[o, :radial, :] = w1_ref[2 * width :, :]
        w_mix[o, radial:, :] = jnp.dot(
            g_ref[o], w1_ref[width : 2 * width, :], preferred_element_type=f32
        ).astype(bf16)
        return carry

    lax.fori_loop(0, nz, project, 0)
    for a in range(1, na):
        for step in range(nz):

            def last(zz, a=a):
                for b in (1, place.b_first, place.b_second):
                    arrival(a, b, zz)

            for entry in rounds[step]:
                when(entry, last)
    table[(nz + 1) * group : (nz + 2) * group, :] = table[group : 2 * group, :]
    table[:group, :] = table[nz * group : (nz + 1) * group, :]
    edges(1, lambda copy: copy.wait_recv())
    window = -(-3 * group // lanes) * lanes
    lane_s = lax.broadcasted_iota(jnp.int32, (slots, lanes), 1).astype(f32)
    sublane = lax.broadcasted_iota(jnp.int32, (atoms, slots), 0).astype(f32)

    def domain(o):
        turned = [jnp.broadcast_to(mg_ref[o, q : q + 1, :], (lanes, lanes)).T for q in range(2 * parts)]
        position = jnp.concatenate(turned[:parts], axis=0)
        target = jnp.concatenate(turned[parts:], axis=0)
        own = g_ref[o]
        pick = (position == lane_s).astype(bf16)
        source = jnp.dot(pick, own, preferred_element_type=f32)
        picks = jnp.concatenate(
            [(position - float(atoms + j * lanes) == lane_s).astype(bf16) for j in range(window // lanes)],
            axis=1,
        )
        rows = table[pl.ds(pl.multiple_of(o * group, 16), window), :]
        source = source + jnp.dot(picks, rows, preferred_element_type=f32)
        mix = jnp.concatenate([bg_ref[o], (target == lane_s).astype(bf16)], axis=1)
        pre = jnp.dot(source.astype(bf16), w1_ref[:width, :], preferred_element_type=f32)
        pre = pre + jnp.dot(mix, w_mix[o], preferred_element_type=f32)
        half = 0.5 * pre
        hidden = (half + half * jnp.tanh(half)).astype(bf16)
        goal = [jnp.broadcast_to(mg_ref[o, q : q + 1, :], (atoms, lanes)) for q in range(parts, 2 * parts)]
        incidence = (jnp.concatenate(goal, axis=1) == sublane).astype(bf16)
        summed = jnp.dot(incidence, hidden, preferred_element_type=f32).astype(bf16)
        return jnp.dot(summed, w2_ref[...], preferred_element_type=f32)

    routes = [sorted((o for o in range(nz) if o != me), key=lambda o: (0 < o < nz - 1, abs(o - me)) if 0 < me < nz - 1 else -abs(o - me)) for me in range(nz)]

    def target_of(step):
        o = 0
        for me in range(nz):
            for k in range(nz - 1):
                o = o + jnp.where((z == me) & (step == k), routes[me][k], 0)
        return o

    def returned(step):
        device = place.along_z(step + 1)
        return remote(part_ref.at[step], landed.at[step], p_send.at[step], p_receive.at[step], device)

    def other(step, carry):
        o = target_of(step)
        slot = lax.rem(o - z + nz - 1, nz)
        part_ref[slot] = domain(o).astype(bf16)
        returned(slot).start()
        return carry

    lax.fori_loop(0, nz - 1, other, 0)
    total = domain(z)
    for step in range(nz - 1):
        returned(step).wait_recv()
        total = total + landed[step].astype(f32)
    mean_square = jnp.mean(total * total, axis=-1, keepdims=True)
    normed = (total * lax.rsqrt(mean_square + 1e-05)).astype(bf16)
    update = jnp.dot(normed, w3_ref[...], preferred_element_type=f32)
    new_rows = (f_ref[...].astype(f32) + update).astype(bf16)
    edge_rows[...] = boundary(meta_ref[0, 2 * parts : 2 * parts + 1, :], new_rows)

    started = []

    def begin(b, c, k, kind, slot, device):
        index = 1 if b is None else b
        rows = pl.ds(0, halo) if k is None else pl.ds(k * n_rows, n_rows)
        if b is None and isinstance(c, int):
            source = edge_rows.at[rows]
        else:
            source = out_ref.at[0, index, c, rows]
        k = 0 if k is None else k
        copy = remote(source, out_ref.at[(*slot, rows)], n_send.at[kind, index, c, k], n_receive.at[(*slot, k)], device)
        copy.start()
        started.append(copy)

    def landing(a, b, c, k=None):
        rows = pl.ds(0, halo) if k is None else pl.ds(k * n_rows, n_rows)
        there = out_ref.at[a, b, c, rows]
        remote(there, there, n_send.at[0, 0, 0, 0], n_receive.at[a, b, c, 0 if k is None else k], place.first).wait_recv()

    def to_siblings_next(b, c):
        for i, device in enumerate(place.siblings):
            begin(b, c, None, 4 + i, (place.sibling_slot(i), 1 if b is None else b, c), device)

    for k in range(chunks_next):
        begin(None, 1, k, 0, (0, 1, 0), place.along_z(1))
        begin(None, 1, k, 1, (0, 1, 2), place.along_z(-1))
    for k in range(chunks_next):
        begin(None, 1, k, 3, (0, place.b_first, 1), place.diagonal)
    for k in range(chunks_next):
        begin(None, 1, k, 2, (0, place.b_second, 1), place.first)
    to_siblings_next(None, 1)
    centre = pltpu.make_async_copy(edge_rows, out_ref.at[0, 1, 1], local.at[0])
    centre.start()
    fresh[...] = new_rows
    keep = pltpu.make_async_copy(fresh, new_ref, local.at[1])
    keep.start()
    near = jnp.where(z == 0, 2, 0)
    order = (1, near, 2 - near)

    def own_next(c):
        for k in range(chunks_next):
            landing(0, 1, c, k)
            begin(None, c, k, 2, (0, place.b_second, c), place.first)
        to_siblings_next(None, c)

    def other_next(b, c):
        for k in range(chunks_next):
            landing(0, b, c, k)
            if b is place.b_second and isinstance(c, int):
                begin(b, c, k, 0, (0, b, 0), place.along_z(1))
                begin(b, c, k, 1, (0, b, 2), place.along_z(-1))
        to_siblings_next(b, c)

    own_next(order[1])
    other_next(place.b_second, 1)
    own_next(order[2])
    for c in order:
        other_next(place.b_first, c)
    for c in order[1:]:
        other_next(place.b_second, c)
    for b in (1, place.b_first, place.b_second):
        for a in range(1, na):
            for c in order:
                landing(a, b, c)
    for group_ in rounds:
        for entry in group_:
            own_stage(entry, finish)
            first_stage(entry, finish)
            second_stage(entry, finish)
    for q in range(2):
        edges(q, finish)
    for step in range(nz - 1):
        returned(step).wait_send()
    for copy in started:
        copy.wait_send()
    keep.wait()
    centre.wait()


def spread_kernel(new_ref, blocks_ref, new_out, out_ref, row_sem, out_sem):
    na = blocks_ref.shape[0]
    parts = (1, 0, 1) if na == 2 else (2, 0, 1)
    stores = [pltpu.make_async_copy(new_ref, new_out, row_sem.at[0])]
    stores[0].start()
    for part, slot in enumerate(parts):
        for b in range(3):
            for c in range(3):
                cell = part * 9 + b * 3 + c
                if cell != 13:
                    cell = cell - 1 if cell > 13 else cell
                    stores.append(pltpu.make_async_copy(blocks_ref.at[slot, b, c], out_ref.at[cell], out_sem.at[cell]))
                    stores[-1].start()
    for copy in stores:
        copy.wait()


def shards(sizes, features, halo_index, edge_src, edge_dst, edge_count, edge_basis, w_edge_in, w_edge_out, w_update):
    nx, ny, nz = sizes
    atoms, width = features.shape
    groups, slots = edge_src.shape
    halo = halo_index.shape[0]
    radial = edge_basis.shape[1]
    hidden = w_edge_in.shape[2]
    lanes = -(-max(atoms, halo) // 128) * 128
    na = 2 if nx == 2 else 3
    f32, bf16 = jnp.float32, jnp.bfloat16
    basis = edge_basis.reshape(groups, slots, radial)
    anywhere = pl.BlockSpec(memory_space=pl.ANY)
    dma = pltpu.SemaphoreType.DMA
    chunks = 1
    pieces = 1
    chunks_next = 1
    meta_rows = -(-(2 * (slots // lanes) + 1) // 8) * 8
    hbm = functools.partial(pltpu.with_memory_space_constraint, memory_space=pltpu.HBM)
    group = na * 3 * halo
    window = -(-3 * group // lanes) * lanes
    table_rows = (nz - 1) * group + window
    new_rows, blocks = pl.pallas_call(
        functools.partial(layer_kernel, sizes),
        out_shape=(
            pltpu.VMEM((atoms, width), bf16),
            pltpu.VMEM((na, 3, 3, halo, width), bf16),
        ),
        in_specs=[anywhere] * 9,
        out_specs=(anywhere, anywhere),
        scratch_shapes=[
            pltpu.VMEM((atoms, width), bf16),
            pltpu.VMEM((1, halo), jnp.int32),
            pltpu.VMEM((groups, slots), jnp.int32),
            pltpu.VMEM((groups, slots), jnp.int32),
            pltpu.SMEM((groups,), jnp.int32),
            pltpu.VMEM((nz, meta_rows, lanes), f32),
            pltpu.VMEM((nz, atoms, width), bf16),
            pltpu.VMEM((nz, slots, radial), bf16),
            pltpu.VMEM((nz, meta_rows, lanes), f32),
            pltpu.VMEM(w_edge_in.shape[1:], bf16),
            pltpu.VMEM(w_edge_out.shape[1:], bf16),
            pltpu.VMEM(w_update.shape, bf16),
            pltpu.VMEM((table_rows, width), bf16),
            pltpu.VMEM((nz, radial + lanes, hidden), bf16),
            pltpu.VMEM((nz - 1, atoms, width), bf16),
            pltpu.VMEM((nz - 1, atoms, width), bf16),
            pltpu.VMEM((halo, width), bf16),
            pltpu.VMEM((atoms, width), bf16),
            dma((2, nz, pieces)),
            dma((nz, pieces)),
            dma((3, nz, chunks)),
            dma((na, 3, nz, chunks)),
            dma((na - 1, 3, nz)),
            dma((2, nz)),
            dma((2, nz)),
            dma((9,)),
            dma((nz - 1,)),
            dma((nz - 1,)),
            dma((4 + na - 1, 3, 3, chunks_next)),
            dma((na, 3, 3, chunks_next)),
        ],
        compiler_params=pltpu.CompilerParams(
            collective_id=0, has_side_effects=True, vmem_limit_bytes=56 * 1024 * 1024
        ),
        name="layer",
    )(*(hbm(array) for array in (features, halo_index.reshape(1, halo), edge_src, edge_dst, edge_count, basis,
                                  w_edge_in[0], w_edge_out[0], w_update)))
    blocks = pltpu.with_memory_space_constraint(blocks, pltpu.VMEM)
    new_rows = pltpu.with_memory_space_constraint(new_rows, pltpu.VMEM)
    return pl.pallas_call(
        spread_kernel,
        out_shape=(
            jax.ShapeDtypeStruct((atoms, width), bf16),
            jax.ShapeDtypeStruct((26, halo, width), bf16),
        ),
        in_specs=[anywhere, anywhere],
        out_specs=(anywhere, anywhere),
        scratch_shapes=[
            dma((1,)),
            dma((26,)),
        ],
        name="spread",
    )(new_rows, blocks)


def solution(mesh):
    sizes = tuple(mesh.shape[name] for name in AXES)
    in_specs = (
        P(AXES, None),
        P(AXES),
        P(AXES, None),
        P(AXES, None),
        P(AXES),
        P(AXES, None),
        P("gz", None, None),
        P("gz", None, None),
        P(),
    )
    out_specs = (P(AXES, None), P(AXES, None, None))
    return jax.shard_map(
        functools.partial(shards, sizes), mesh=mesh, in_specs=in_specs, out_specs=out_specs, check_vma=False
    )
```

```python
import functools

import jax
import jax.numpy as jnp
from jax import lax
from jax.experimental import pallas as pl
from jax.experimental.pallas import tpu as pltpu
from jax.sharding import PartitionSpec as P

AXES = ("gx", "gy", "gz")
MESH = pl.DeviceIdType.MESH


class Place:
    def __init__(self, sizes):
        self.nx, self.ny, self.nz = sizes
        self.x, self.y, self.z = (lax.axis_index(name) for name in AXES)
        x, y, z = self.x, self.y, self.z
        self.first = (x, y + 1 - 2 * lax.rem(y, 2), z)
        self.second = (x, lax.rem(y + 2, 4), z)
        self.diagonal = (x, lax.rem(y + 3 - 2 * lax.rem(y, 2), 4), z)
        self.b_first = 2 - 2 * lax.rem(y, 2)
        self.b_second = 2 * lax.rem(y, 2)
        self.siblings = [(lax.rem(x + 1, self.nx), y, z)]
        if self.nx > 2:
            self.siblings.append((lax.rem(x + self.nx - 1, self.nx), y, z))

    def along_z(self, step):
        return (self.x, self.y, lax.rem(self.z + step + self.nz, self.nz))

    def sibling_slot(self, index):
        return 1 if self.nx == 2 else 2 - index

    def greet(self):
        self.barrier = pltpu.get_barrier_semaphore()
        partners = [self.along_z(step) for step in range(1, self.nz)]
        partners += [self.first, self.second, self.diagonal] + self.siblings
        for partner in partners:
            pl.semaphore_signal(self.barrier, inc=1, device_id=partner, device_id_type=MESH)
        self.partners = len(partners)

    def meet(self):
        pl.semaphore_wait(self.barrier, self.partners)


def remote(source, target, send, receive, device):
    return pltpu.make_async_remote_copy(
        src_ref=source,
        dst_ref=target,
        send_sem=send,
        recv_sem=receive,
        device_id=device,
        device_id_type=MESH,
    )


def layer_kernel(sizes, f_hbm, index_hbm, src_hbm, dst_hbm, count_hbm, basis_hbm, w1_hbm, w2_hbm, w3_hbm,
                 new_ref, out_ref,
                 f_ref, index_ref, src_ref, dst_ref, count_ref,
                 meta_ref, g_ref, bg_ref, mg_ref, w1_ref, w2_ref, w3_ref, table, w_mix,
                 part_ref, landed, edge_rows, fresh,
                 c_send, c_receive, t_send, t_receive, s_send, e_send, e_receive, local, p_send, p_receive,
                 n_send, n_receive):
    place = Place(sizes)
    z, nz = place.z, place.nz
    halo = index_ref.shape[1]
    na = out_ref.shape[0]
    atoms, width = g_ref.shape[1:]
    groups, slots = src_ref.shape
    radial = bg_ref.shape[2]
    lanes = meta_ref.shape[2]
    parts = slots // lanes
    group = na * 3 * halo
    f32, bf16 = jnp.float32, jnp.bfloat16
    chunks = t_receive.shape[3]
    pieces = c_receive.shape[1]
    f_rows = atoms // pieces
    b_rows = halo // chunks
    chunks_next = n_receive.shape[3]
    n_rows = halo // chunks_next
    edge_pairs = ((meta_ref, mg_ref), (basis_hbm, bg_ref))

    place.greet()
    inputs = [
        pltpu.make_async_copy(source, target, local.at[k])
        for k, (source, target) in enumerate(
            [(src_hbm, src_ref), (dst_hbm, dst_ref), (index_hbm, index_ref), (count_hbm, count_ref), (f_hbm, f_ref)]
        )
    ]
    weights = [
        pltpu.make_async_copy(source, target, local.at[5 + k])
        for k, (source, target) in enumerate(
            [(w1_hbm, w1_ref), (w2_hbm, w2_ref), (w3_hbm, w3_ref), (basis_hbm.at[z], bg_ref.at[z])]
        )
    ]
    for copy in inputs + weights:
        copy.start()
    rest = table.shape[0] - (nz + 2) * group
    table[(nz + 2) * group :, :] = jnp.zeros((rest, width), bf16)
    meta_ref[...] = jnp.zeros_like(meta_ref)
    for copy in inputs:
        copy.wait()
    edge_src = src_ref[...].astype(f32)
    beyond = edge_src - float(atoms)
    offset = jnp.floor((beyond + 0.5) * (1.0 / halo))
    slot = beyond - offset * float(halo)
    offset = jnp.where(offset >= 13.0, offset + 1.0, offset)
    off_x = jnp.floor((offset + 0.5) * (1.0 / 9.0))
    inner = offset - 9.0 * off_x
    off_y = jnp.floor((inner + 0.5) * (1.0 / 3.0))
    off_z = inner - 3.0 * off_y
    slot_x = jnp.where(off_x == 1.0, 0.0, jnp.where(off_x == 2.0, 1.0, float(na - 1)))
    position = float(atoms) + ((off_z * float(na) + slot_x) * 3.0 + off_y) * float(halo) + slot
    position = jnp.where(edge_src < float(atoms), edge_src, position)
    row_lane = lax.broadcasted_iota(jnp.int32, (1, slots), 1)
    index_row = index_ref[...].astype(f32)
    for j in range(groups):
        target = jnp.where(row_lane < count_ref[j], dst_ref[j : j + 1, :], -1).astype(f32)
        for q in range(parts):
            meta_ref[j, q : q + 1, :] = position[j : j + 1, q * lanes : (q + 1) * lanes]
            meta_ref[j, parts + q : parts + q + 1, :] = target[:, q * lanes : (q + 1) * lanes]
        meta_ref[j, 2 * parts : 2 * parts + 1, :halo] = index_row
    g_ref[z] = f_ref[...]
    mg_ref[z] = meta_ref[z]

    def when(entry, action):
        s, sign = entry
        zz = z + sign * s
        if s == 0:
            action(zz)
        else:
            pl.when((zz >= 0) & (zz < nz))(functools.partial(action, zz))

    def feature(zz, k):
        return g_ref.at[zz, pl.ds(k * f_rows, f_rows)]

    def row_of(a, b, zz):
        return pl.multiple_of(((zz + 1) * (na * 3) + a * 3 + b) * halo, 16)

    def block(a, b, zz, k=None):
        if k is None:
            return table.at[pl.ds(row_of(a, b, zz), halo)]
        return table.at[pl.ds(pl.multiple_of(row_of(a, b, zz) + k * b_rows, 16), b_rows)]

    def arrival(a, b, zz, k=None):
        there = block(a, b, zz, k)
        k = 0 if k is None else k
        remote(there, there, t_send.at[0, 0, 0], t_receive.at[a, b, zz, k], place.first).wait_recv()

    def chain(entry, zz, k, do):
        s, sign = entry
        if s < nz - 1:
            for go in ((1, -1) if s == 0 else (-sign,)):
                device = (place.x, place.y, z + go)

                def act():
                    way = 0 if go > 0 else 1
                    do(remote(feature(zz, k), feature(zz, k), c_send.at[way, zz, k], c_receive.at[zz, k], device))

                pl.when((z + go >= 0) & (z + go < nz))(act)

    def to_siblings(b, zz, do):
        for i, device in enumerate(place.siblings):
            do(remote(block(0, b, zz), block(place.sibling_slot(i), b, zz), s_send.at[i, b, zz],
                      t_receive.at[place.sibling_slot(i), b, zz, 0], device))

    def pass_on(b, zz, k, which, do):
        device = (place.first, place.second, place.diagonal)[which]
        slot = place.b_first if which == 2 else place.b_second
        do(remote(block(0, b, zz, k), block(0, slot, zz, k), t_send.at[which, zz, k],
                  t_receive.at[0, slot, zz, k], device))

    lane = lax.broadcasted_iota(jnp.int32, (lanes, lanes), 1).astype(f32)

    def boundary(index_row, rows):
        index = jnp.broadcast_to(index_row, (lanes, lanes)).T
        pick = (index == lane).astype(bf16)[:halo, :atoms]
        return jnp.dot(pick, rows, preferred_element_type=f32).astype(bf16)

    table[pl.ds(row_of(0, 1, z), halo), :] = boundary(meta_ref[0, 2 * parts : 2 * parts + 1, :], f_ref[...])
    place.meet()

    def own_stage(entry, do):
        s, sign = entry

        def act(zz):
            for k in range(pieces):
                if s > 0 and do is start:
                    remote(feature(zz, k), feature(zz, k), c_send.at[0, 0, 0], c_receive.at[zz, k], place.first).wait_recv()
                chain(entry, zz, k, do)
            if s > 0 and do is start:
                edge(0, s if sign < 0 else nz - s, lambda copy: copy.wait_recv())
                table[pl.ds(row_of(0, 1, zz), halo), :] = boundary(mg_ref[zz, 2 * parts : 2 * parts + 1, :], g_ref[zz])
            for k in range(chunks):
                pass_on(1, zz, k, 0, do)
                if s in straight:
                    pass_on(1, zz, k, 2, do)
            to_siblings(1, zz, do)

        when(entry, act)

    def first_stage(entry, do):
        def act(zz):
            for k in range(chunks):
                if do is start:
                    arrival(0, place.b_first, zz, k)
                if entry[0] not in straight:
                    pass_on(place.b_first, zz, k, 1, do)
            to_siblings(place.b_first, zz, do)

        when(entry, act)

    def second_stage(entry, do):
        def act(zz):
            if do is start:
                for k in range(chunks):
                    arrival(0, place.b_second, zz, k)
            to_siblings(place.b_second, zz, do)

        when(entry, act)

    def edge(q, step, do):
        own, grid = edge_pairs[q]
        device = place.along_z(step)
        do(remote(own.at[device[2]], grid.at[z], e_send.at[q, step], e_receive.at[q, step], device))

    def edges(q, do):
        for step in range(1, nz):
            edge(q, step, do)

    def basis(ends):
        for step in range(1, nz):
            goal = lax.rem(z + step, nz)
            last = (goal == 0) | (goal == nz - 1)
            pl.when(last if ends else jnp.logical_not(last))(functools.partial(edge, 1, step, start))

    def start(copy):
        copy.start()

    def finish(copy):
        copy.wait_send()

    straight = ()
    rounds = [[(0, 0)]] + [[(s, -1), (s, 1)] for s in range(1, nz)]
    for r in range(nz + 2):
        if r < nz:
            for entry in rounds[r]:
                own_stage(entry, start)
        if r == 0:
            edges(0, start)
        if r == nz - 1:
            basis(False)
        if r == nz:
            basis(True)
        if 1 <= r <= nz:
            for entry in rounds[r - 1]:
                first_stage(entry, start)
        if r >= 2:
            for entry in rounds[r - 2]:
                second_stage(entry, start)
    for copy in weights:
        copy.wait()

    def project(o, carry):
        w_mix[o, :radial, :] = w1_ref[2 * width :, :]
        w_mix[o, radial:, :] = jnp.dot(
            g_ref[o], w1_ref[width : 2 * width, :], preferred_element_type=f32
        ).astype(bf16)
        return carry

    lax.fori_loop(0, nz, project, 0)
    for a in range(1, na):
        for step in range(nz):

            def last(zz, a=a):
                for b in (1, place.b_first, place.b_second):
                    arrival(a, b, zz)

            for entry in rounds[step]:
                when(entry, last)
    table[(nz + 1) * group : (nz + 2) * group, :] = table[group : 2 * group, :]
    table[:group, :] = table[nz * group : (nz + 1) * group, :]
    edges(1, lambda copy: copy.wait_recv())
    window = -(-3 * group // lanes) * lanes
    lane_s = lax.broadcasted_iota(jnp.int32, (slots, lanes), 1).astype(f32)
    sublane = lax.broadcasted_iota(jnp.int32, (atoms, slots), 0).astype(f32)

    def domain(o):
        turned = [jnp.broadcast_to(mg_ref[o, q : q + 1, :], (lanes, lanes)).T for q in range(2 * parts)]
        position = jnp.concatenate(turned[:parts], axis=0)
        target = jnp.concatenate(turned[parts:], axis=0)
        own = g_ref[o]
        pick = (position == lane_s).astype(bf16)
        source = jnp.dot(pick, own, preferred_element_type=f32)
        picks = jnp.concatenate(
            [(position - float(atoms + j * lanes) == lane_s).astype(bf16) for j in range(window // lanes)],
            axis=1,
        )
        rows = table[pl.ds(pl.multiple_of(o * group, 16), window), :]
        source = source + jnp.dot(picks, rows, preferred_element_type=f32)
        mix = jnp.concatenate([bg_ref[o], (target == lane_s).astype(bf16)], axis=1)
        pre = jnp.dot(source.astype(bf16), w1_ref[:width, :], preferred_element_type=f32)
        pre = pre + jnp.dot(mix, w_mix[o], preferred_element_type=f32)
        half = 0.5 * pre
        hidden = (half + half * jnp.tanh(half)).astype(bf16)
        goal = [jnp.broadcast_to(mg_ref[o, q : q + 1, :], (atoms, lanes)) for q in range(parts, 2 * parts)]
        incidence = (jnp.concatenate(goal, axis=1) == sublane).astype(bf16)
        summed = jnp.dot(incidence, hidden, preferred_element_type=f32).astype(bf16)
        return jnp.dot(summed, w2_ref[...], preferred_element_type=f32)

    routes = [sorted((o for o in range(nz) if o != me), key=lambda o: (0 < o < nz - 1, abs(o - me)) if 0 < me < nz - 1 else -abs(o - me)) for me in range(nz)]

    def target_of(step):
        o = 0
        for me in range(nz):
            for k in range(nz - 1):
                o = o + jnp.where((z == me) & (step == k), routes[me][k], 0)
        return o

    def returned(step):
        device = place.along_z(step + 1)
        return remote(part_ref.at[step], landed.at[step], p_send.at[step], p_receive.at[step], device)

    def other(step, carry):
        o = target_of(step)
        slot = lax.rem(o - z + nz - 1, nz)
        part_ref[slot] = domain(o).astype(bf16)
        returned(slot).start()
        return carry

    lax.fori_loop(0, nz - 1, other, 0)
    total = domain(z)
    for group_ in rounds:
        for entry in group_:
            own_stage(entry, finish)
            first_stage(entry, finish)
            second_stage(entry, finish)
    for q in range(2):
        edges(q, finish)
    for step in range(nz - 1):
        returned(step).wait_recv()
        total = total + landed[step].astype(f32)
    mean_square = jnp.mean(total * total, axis=-1, keepdims=True)
    normed = (total * lax.rsqrt(mean_square + 1e-05)).astype(bf16)
    update = jnp.dot(normed, w3_ref[...], preferred_element_type=f32)
    new_rows = (f_ref[...].astype(f32) + update).astype(bf16)
    edge_rows[...] = boundary(meta_ref[0, 2 * parts : 2 * parts + 1, :], new_rows)

    started = []

    def begin(b, c, k, kind, slot, device):
        index = 1 if b is None else b
        rows = pl.ds(0, halo) if k is None else pl.ds(k * n_rows, n_rows)
        if b is None and isinstance(c, int):
            source = edge_rows.at[rows]
        else:
            source = out_ref.at[0, index, c, rows]
        k = 0 if k is None else k
        copy = remote(source, out_ref.at[(*slot, rows)], n_send.at[kind, index, c, k], n_receive.at[(*slot, k)], device)
        copy.start()
        started.append(copy)
        return copy

    def landing(a, b, c, k=None):
        rows = pl.ds(0, halo) if k is None else pl.ds(k * n_rows, n_rows)
        there = out_ref.at[a, b, c, rows]
        remote(there, there, n_send.at[0, 0, 0, 0], n_receive.at[a, b, c, 0 if k is None else k], place.first).wait_recv()

    def to_siblings_next(b, c):
        for i, device in enumerate(place.siblings):
            begin(b, c, None, 4 + i, (place.sibling_slot(i), 1 if b is None else b, c), device)

    away = jnp.where(z == nz - 1, 1, -1)
    at_end = (z == 0) | (z == nz - 1)
    for k in range(chunks_next):
        begin(None, 1, k, 0, (0, 1, 0), place.along_z(1))
        begin(None, 1, k, 1, (0, 1, 2), place.along_z(-1))
    to_diagonal = [begin(None, 1, k, 3, (0, place.b_first, 1), place.diagonal) for k in range(chunks_next)]
    for k in range(chunks_next):
        begin(None, 1, k, 2, (0, place.b_second, 1), place.first)
    to_siblings_next(None, 1)
    centre = pltpu.make_async_copy(edge_rows, out_ref.at[0, 1, 1], local.at[0])
    centre.start()
    fresh[...] = new_rows
    keep = pltpu.make_async_copy(fresh, new_ref, local.at[1])
    keep.start()
    for step in range(nz - 1):
        returned(step).wait_send()
    near = jnp.where(z == 0, 2, 0)
    order = (1, near, 2 - near)

    def own_next(c):
        for k in range(chunks_next):
            landing(0, 1, c, k)
            begin(None, c, k, 2, (0, place.b_second, c), place.first)
        to_siblings_next(None, c)

    def other_next(b, c):
        for k in range(chunks_next):
            landing(0, b, c, k)
            if b is place.b_second and isinstance(c, int):
                begin(b, c, k, 0, (0, b, 0), place.along_z(1))
                begin(b, c, k, 1, (0, b, 2), place.along_z(-1))
        to_siblings_next(b, c)

    own_next(order[1])
    other_next(place.b_second, 1)
    own_next(order[2])
    for c in order:
        other_next(place.b_first, c)
    for c in order[1:]:
        other_next(place.b_second, c)
    for b in (1, place.b_first, place.b_second):
        for a in range(1, na):
            for c in order:
                landing(a, b, c)
    for copy in started:
        copy.wait_send()
    keep.wait()
    centre.wait()


def spread_kernel(new_ref, blocks_ref, new_out, out_ref, row_sem, out_sem):
    na = blocks_ref.shape[0]
    parts = (1, 0, 1) if na == 2 else (2, 0, 1)
    stores = [pltpu.make_async_copy(new_ref, new_out, row_sem.at[0])]
    stores[0].start()
    for part, slot in enumerate(parts):
        for b in range(3):
            for c in range(3):
                cell = part * 9 + b * 3 + c
                if cell != 13:
                    cell = cell - 1 if cell > 13 else cell
                    stores.append(pltpu.make_async_copy(blocks_ref.at[slot, b, c], out_ref.at[cell], out_sem.at[cell]))
                    stores[-1].start()
    for copy in stores:
        copy.wait()


def shards(sizes, features, halo_index, edge_src, edge_dst, edge_count, edge_basis, w_edge_in, w_edge_out, w_update):
    nx, ny, nz = sizes
    atoms, width = features.shape
    groups, slots = edge_src.shape
    halo = halo_index.shape[0]
    radial = edge_basis.shape[1]
    hidden = w_edge_in.shape[2]
    lanes = -(-max(atoms, halo) // 128) * 128
    na = 2 if nx == 2 else 3
    f32, bf16 = jnp.float32, jnp.bfloat16
    basis = edge_basis.reshape(groups, slots, radial)
    anywhere = pl.BlockSpec(memory_space=pl.ANY)
    dma = pltpu.SemaphoreType.DMA
    chunks = 1
    pieces = 1
    chunks_next = 1
    meta_rows = -(-(2 * (slots // lanes) + 1) // 8) * 8
    hbm = functools.partial(pltpu.with_memory_space_constraint, memory_space=pltpu.HBM)
    group = na * 3 * halo
    window = -(-3 * group // lanes) * lanes
    table_rows = (nz - 1) * group + window
    new_rows, blocks = pl.pallas_call(
        functools.partial(layer_kernel, sizes),
        out_shape=(
            pltpu.VMEM((atoms, width), bf16),
            pltpu.VMEM((na, 3, 3, halo, width), bf16),
        ),
        in_specs=[anywhere] * 9,
        out_specs=(anywhere, anywhere),
        scratch_shapes=[
            pltpu.VMEM((atoms, width), bf16),
            pltpu.VMEM((1, halo), jnp.int32),
            pltpu.VMEM((groups, slots), jnp.int32),
            pltpu.VMEM((groups, slots), jnp.int32),
            pltpu.SMEM((groups,), jnp.int32),
            pltpu.VMEM((nz, meta_rows, lanes), f32),
            pltpu.VMEM((nz, atoms, width), bf16),
            pltpu.VMEM((nz, slots, radial), bf16),
            pltpu.VMEM((nz, meta_rows, lanes), f32),
            pltpu.VMEM(w_edge_in.shape[1:], bf16),
            pltpu.VMEM(w_edge_out.shape[1:], bf16),
            pltpu.VMEM(w_update.shape, bf16),
            pltpu.VMEM((table_rows, width), bf16),
            pltpu.VMEM((nz, radial + lanes, hidden), bf16),
            pltpu.VMEM((nz - 1, atoms, width), bf16),
            pltpu.VMEM((nz - 1, atoms, width), bf16),
            pltpu.VMEM((halo, width), bf16),
            pltpu.VMEM((atoms, width), bf16),
            dma((2, nz, pieces)),
            dma((nz, pieces)),
            dma((3, nz, chunks)),
            dma((na, 3, nz, chunks)),
            dma((na - 1, 3, nz)),
            dma((2, nz)),
            dma((2, nz)),
            dma((9,)),
            dma((nz - 1,)),
            dma((nz - 1,)),
            dma((4 + na - 1, 3, 3, chunks_next)),
            dma((na, 3, 3, chunks_next)),
        ],
        compiler_params=pltpu.CompilerParams(
            collective_id=0, has_side_effects=True, vmem_limit_bytes=56 * 1024 * 1024
        ),
        name="layer",
    )(*(hbm(array) for array in (features, halo_index.reshape(1, halo), edge_src, edge_dst, edge_count, basis,
                                  w_edge_in[0], w_edge_out[0], w_update)))
    blocks = pltpu.with_memory_space_constraint(blocks, pltpu.VMEM)
    new_rows = pltpu.with_memory_space_constraint(new_rows, pltpu.VMEM)
    return pl.pallas_call(
        spread_kernel,
        out_shape=(
            jax.ShapeDtypeStruct((atoms, width), bf16),
            jax.ShapeDtypeStruct((26, halo, width), bf16),
        ),
        in_specs=[anywhere, anywhere],
        out_specs=(anywhere, anywhere),
        scratch_shapes=[
            dma((1,)),
            dma((26,)),
        ],
        name="spread",
    )(new_rows, blocks)


def solution(mesh):
    sizes = tuple(mesh.shape[name] for name in AXES)
    in_specs = (
        P(AXES, None),
        P(AXES),
        P(AXES, None),
        P(AXES, None),
        P(AXES),
        P(AXES, None),
        P("gz", None, None),
        P("gz", None, None),
        P(),
    )
    out_specs = (P(AXES, None), P(AXES, None, None))
    return jax.shard_map(
        functools.partial(shards, sizes), mesh=mesh, in_specs=in_specs, out_specs=out_specs, check_vma=False
    )
```

```python
import functools

import jax
import jax.numpy as jnp
from jax import lax
from jax.experimental import pallas as pl
from jax.experimental.pallas import tpu as pltpu
from jax.sharding import PartitionSpec as P

AXES = ("gx", "gy", "gz")
MESH = pl.DeviceIdType.MESH


class Place:
    def __init__(self, sizes):
        self.nx, self.ny, self.nz = sizes
        self.x, self.y, self.z = (lax.axis_index(name) for name in AXES)
        x, y, z = self.x, self.y, self.z
        self.first = (x, y + 1 - 2 * lax.rem(y, 2), z)
        self.second = (x, lax.rem(y + 2, 4), z)
        self.diagonal = (x, lax.rem(y + 3 - 2 * lax.rem(y, 2), 4), z)
        self.b_first = 2 - 2 * lax.rem(y, 2)
        self.b_second = 2 * lax.rem(y, 2)
        self.siblings = [(lax.rem(x + 1, self.nx), y, z)]
        if self.nx > 2:
            self.siblings.append((lax.rem(x + self.nx - 1, self.nx), y, z))

    def along_z(self, step):
        return (self.x, self.y, lax.rem(self.z + step + self.nz, self.nz))

    def sibling_slot(self, index):
        return 1 if self.nx == 2 else 2 - index

    def greet(self):
        self.barrier = pltpu.get_barrier_semaphore()
        partners = [self.along_z(step) for step in range(1, self.nz)]
        partners += [self.first, self.second, self.diagonal] + self.siblings
        for partner in partners:
            pl.semaphore_signal(self.barrier, inc=1, device_id=partner, device_id_type=MESH)
        self.partners = len(partners)

    def meet(self):
        pl.semaphore_wait(self.barrier, self.partners)


def remote(source, target, send, receive, device):
    return pltpu.make_async_remote_copy(
        src_ref=source,
        dst_ref=target,
        send_sem=send,
        recv_sem=receive,
        device_id=device,
        device_id_type=MESH,
    )


def layer_kernel(sizes, f_hbm, index_hbm, src_hbm, dst_hbm, count_hbm, basis_hbm, w1_hbm, w2_hbm, w3_hbm,
                 new_ref, out_ref,
                 f_ref, index_ref, src_ref, dst_ref, count_ref,
                 meta_ref, g_ref, bg_ref, mg_ref, w1_ref, w2_ref, w3_ref, table, w_mix,
                 part_ref, landed, edge_rows, fresh,
                 c_send, c_receive, t_send, t_receive, s_send, e_send, e_receive, local, p_send, p_receive,
                 n_send, n_receive):
    place = Place(sizes)
    z, nz = place.z, place.nz
    halo = index_ref.shape[1]
    na = out_ref.shape[0]
    atoms, width = g_ref.shape[1:]
    groups, slots = src_ref.shape
    radial = bg_ref.shape[2]
    lanes = meta_ref.shape[2]
    parts = slots // lanes
    group = na * 3 * halo
    f32, bf16 = jnp.float32, jnp.bfloat16
    chunks = t_receive.shape[3]
    pieces = c_receive.shape[1]
    f_rows = atoms // pieces
    b_rows = halo // chunks
    chunks_next = n_receive.shape[3]
    n_rows = halo // chunks_next
    edge_pairs = ((meta_ref, mg_ref), (basis_hbm, bg_ref))

    place.greet()
    inputs = [
        pltpu.make_async_copy(source, target, local.at[k])
        for k, (source, target) in enumerate(
            [(src_hbm, src_ref), (dst_hbm, dst_ref), (index_hbm, index_ref), (count_hbm, count_ref), (f_hbm, f_ref)]
        )
    ]
    weights = [
        pltpu.make_async_copy(source, target, local.at[5 + k])
        for k, (source, target) in enumerate(
            [(w1_hbm, w1_ref), (w2_hbm, w2_ref), (w3_hbm, w3_ref), (basis_hbm.at[z], bg_ref.at[z])]
        )
    ]
    for copy in inputs + weights:
        copy.start()
    rest = table.shape[0] - (nz + 2) * group
    table[(nz + 2) * group :, :] = jnp.zeros((rest, width), bf16)
    meta_ref[...] = jnp.zeros_like(meta_ref)
    for copy in inputs:
        copy.wait()
    edge_src = src_ref[...].astype(f32)
    beyond = edge_src - float(atoms)
    offset = jnp.floor((beyond + 0.5) * (1.0 / halo))
    slot = beyond - offset * float(halo)
    offset = jnp.where(offset >= 13.0, offset + 1.0, offset)
    off_x = jnp.floor((offset + 0.5) * (1.0 / 9.0))
    inner = offset - 9.0 * off_x
    off_y = jnp.floor((inner + 0.5) * (1.0 / 3.0))
    off_z = inner - 3.0 * off_y
    slot_x = jnp.where(off_x == 1.0, 0.0, jnp.where(off_x == 2.0, 1.0, float(na - 1)))
    position = float(atoms) + ((off_z * float(na) + slot_x) * 3.0 + off_y) * float(halo) + slot
    position = jnp.where(edge_src < float(atoms), edge_src, position)
    row_lane = lax.broadcasted_iota(jnp.int32, (1, slots), 1)
    index_row = index_ref[...].astype(f32)
    for j in range(groups):
        target = jnp.where(row_lane < count_ref[j], dst_ref[j : j + 1, :], -1).astype(f32)
        for q in range(parts):
            meta_ref[j, q : q + 1, :] = position[j : j + 1, q * lanes : (q + 1) * lanes]
            meta_ref[j, parts + q : parts + q + 1, :] = target[:, q * lanes : (q + 1) * lanes]
        meta_ref[j, 2 * parts : 2 * parts + 1, :halo] = index_row
    g_ref[z] = f_ref[...]
    mg_ref[z] = meta_ref[z]

    def when(entry, action):
        s, sign = entry
        zz = z + sign * s
        if s == 0:
            action(zz)
        else:
            pl.when((zz >= 0) & (zz < nz))(functools.partial(action, zz))

    def feature(zz, k):
        return g_ref.at[zz, pl.ds(k * f_rows, f_rows)]

    def row_of(a, b, zz):
        return pl.multiple_of(((zz + 1) * (na * 3) + a * 3 + b) * halo, 16)

    def block(a, b, zz, k=None):
        if k is None:
            return table.at[pl.ds(row_of(a, b, zz), halo)]
        return table.at[pl.ds(pl.multiple_of(row_of(a, b, zz) + k * b_rows, 16), b_rows)]

    def arrival(a, b, zz, k=None):
        there = block(a, b, zz, k)
        k = 0 if k is None else k
        remote(there, there, t_send.at[0, 0, 0], t_receive.at[a, b, zz, k], place.first).wait_recv()

    def chain(entry, zz, k, do):
        s, sign = entry
        if s < nz - 1:
            for go in ((1, -1) if s == 0 else (-sign,)):
                device = (place.x, place.y, z + go)

                def act():
                    way = 0 if go > 0 else 1
                    do(remote(feature(zz, k), feature(zz, k), c_send.at[way, zz, k], c_receive.at[zz, k], device))

                pl.when((z + go >= 0) & (z + go < nz))(act)

    def to_siblings(b, zz, do):
        for i, device in enumerate(place.siblings):
            do(remote(block(0, b, zz), block(place.sibling_slot(i), b, zz), s_send.at[i, b, zz],
                      t_receive.at[place.sibling_slot(i), b, zz, 0], device))

    def pass_on(b, zz, k, which, do):
        device = (place.first, place.second, place.diagonal)[which]
        slot = place.b_first if which == 2 else place.b_second
        do(remote(block(0, b, zz, k), block(0, slot, zz, k), t_send.at[which, zz, k],
                  t_receive.at[0, slot, zz, k], device))

    lane = lax.broadcasted_iota(jnp.int32, (lanes, lanes), 1).astype(f32)

    def boundary(index_row, rows):
        index = jnp.broadcast_to(index_row, (lanes, lanes)).T
        pick = (index == lane).astype(bf16)[:halo, :atoms]
        return jnp.dot(pick, rows, preferred_element_type=f32).astype(bf16)

    table[pl.ds(row_of(0, 1, z), halo), :] = boundary(meta_ref[0, 2 * parts : 2 * parts + 1, :], f_ref[...])
    place.meet()

    def own_stage(entry, do):
        s, sign = entry

        def act(zz):
            for k in range(pieces):
                if s > 0 and do is start:
                    remote(feature(zz, k), feature(zz, k), c_send.at[0, 0, 0], c_receive.at[zz, k], place.first).wait_recv()
                chain(entry, zz, k, do)
            if s > 0 and do is start:
                edge(0, s if sign < 0 else nz - s, lambda copy: copy.wait_recv())
                table[pl.ds(row_of(0, 1, zz), halo), :] = boundary(mg_ref[zz, 2 * parts : 2 * parts + 1, :], g_ref[zz])
            to_siblings(1, zz, do)
            for k in range(chunks):
                pass_on(1, zz, k, 0, do)
                if s in straight:
                    pass_on(1, zz, k, 2, do)

        when(entry, act)

    def first_stage(entry, do):
        def act(zz):
            for k in range(chunks):
                if do is start:
                    arrival(0, place.b_first, zz, k)
                if entry[0] not in straight:
                    pass_on(place.b_first, zz, k, 1, do)
            to_siblings(place.b_first, zz, do)

        when(entry, act)

    def second_stage(entry, do):
        def act(zz):
            if do is start:
                for k in range(chunks):
                    arrival(0, place.b_second, zz, k)
            to_siblings(place.b_second, zz, do)

        when(entry, act)

    def edge(q, step, do):
        own, grid = edge_pairs[q]
        device = place.along_z(step)
        do(remote(own.at[device[2]], grid.at[z], e_send.at[q, step], e_receive.at[q, step], device))

    def edges(q, do):
        for step in range(1, nz):
            edge(q, step, do)

    def basis(ends):
        for step in range(1, nz):
            goal = lax.rem(z + step, nz)
            last = (goal == 0) | (goal == nz - 1)
            pl.when(last if ends else jnp.logical_not(last))(functools.partial(edge, 1, step, start))

    def start(copy):
        copy.start()

    def finish(copy):
        copy.wait_send()

    straight = ()
    rounds = [[(0, 0)]] + [[(s, -1), (s, 1)] for s in range(1, nz)]
    for r in range(nz + 2):
        if r < nz:
            for entry in rounds[r]:
                own_stage(entry, start)
        if r == 0:
            edges(0, start)
        if r == nz - 1:
            basis(False)
        if r == nz:
            basis(True)
        if 1 <= r <= nz:
            for entry in rounds[r - 1]:
                first_stage(entry, start)
        if r >= 2:
            for entry in rounds[r - 2]:
                second_stage(entry, start)
    for copy in weights:
        copy.wait()

    def project(o, carry):
        w_mix[o, :radial, :] = w1_ref[2 * width :, :]
        w_mix[o, radial:, :] = jnp.dot(
            g_ref[o], w1_ref[width : 2 * width, :], preferred_element_type=f32
        ).astype(bf16)
        return carry

    lax.fori_loop(0, nz, project, 0)
    for a in range(1, na):
        for step in range(nz):

            def last(zz, a=a):
                for b in (1, place.b_first, place.b_second):
                    arrival(a, b, zz)

            for entry in rounds[step]:
                when(entry, last)
    table[(nz + 1) * group : (nz + 2) * group, :] = table[group : 2 * group, :]
    table[:group, :] = table[nz * group : (nz + 1) * group, :]
    edges(1, lambda copy: copy.wait_recv())
    window = -(-3 * group // lanes) * lanes
    lane_s = lax.broadcasted_iota(jnp.int32, (slots, lanes), 1).astype(f32)
    sublane = lax.broadcasted_iota(jnp.int32, (atoms, slots), 0).astype(f32)

    def domain(o):
        turned = [jnp.broadcast_to(mg_ref[o, q : q + 1, :], (lanes, lanes)).T for q in range(2 * parts)]
        position = jnp.concatenate(turned[:parts], axis=0)
        target = jnp.concatenate(turned[parts:], axis=0)
        own = g_ref[o]
        pick = (position == lane_s).astype(bf16)
        source = jnp.dot(pick, own, preferred_element_type=f32)
        picks = jnp.concatenate(
            [(position - float(atoms + j * lanes) == lane_s).astype(bf16) for j in range(window // lanes)],
            axis=1,
        )
        rows = table[pl.ds(pl.multiple_of(o * group, 16), window), :]
        source = source + jnp.dot(picks, rows, preferred_element_type=f32)
        mix = jnp.concatenate([bg_ref[o], (target == lane_s).astype(bf16)], axis=1)
        pre = jnp.dot(source.astype(bf16), w1_ref[:width, :], preferred_element_type=f32)
        pre = pre + jnp.dot(mix, w_mix[o], preferred_element_type=f32)
        half = 0.5 * pre
        hidden = (half + half * jnp.tanh(half)).astype(bf16)
        goal = [jnp.broadcast_to(mg_ref[o, q : q + 1, :], (atoms, lanes)) for q in range(parts, 2 * parts)]
        incidence = (jnp.concatenate(goal, axis=1) == sublane).astype(bf16)
        summed = jnp.dot(incidence, hidden, preferred_element_type=f32).astype(bf16)
        return jnp.dot(summed, w2_ref[...], preferred_element_type=f32)

    routes = [sorted((o for o in range(nz) if o != me), key=lambda o: (0 < o < nz - 1, abs(o - me)) if 0 < me < nz - 1 else -abs(o - me)) for me in range(nz)]

    def target_of(step):
        o = 0
        for me in range(nz):
            for k in range(nz - 1):
                o = o + jnp.where((z == me) & (step == k), routes[me][k], 0)
        return o

    def returned(step):
        device = place.along_z(step + 1)
        return remote(part_ref.at[step], landed.at[step], p_send.at[step], p_receive.at[step], device)

    def other(step, carry):
        o = target_of(step)
        slot = lax.rem(o - z + nz - 1, nz)
        part_ref[slot] = domain(o).astype(bf16)
        returned(slot).start()
        return carry

    lax.fori_loop(0, nz - 1, other, 0)
    total = domain(z)
    for group_ in rounds:
        for entry in group_:
            own_stage(entry, finish)
            first_stage(entry, finish)
            second_stage(entry, finish)
    for q in range(2):
        edges(q, finish)
    for step in range(nz - 1):
        returned(step).wait_recv()
        total = total + landed[step].astype(f32)
    mean_square = jnp.mean(total * total, axis=-1, keepdims=True)
    normed = (total * lax.rsqrt(mean_square + 1e-05)).astype(bf16)
    update = jnp.dot(normed, w3_ref[...], preferred_element_type=f32)
    new_rows = (f_ref[...].astype(f32) + update).astype(bf16)
    edge_rows[...] = boundary(meta_ref[0, 2 * parts : 2 * parts + 1, :], new_rows)

    started = []

    def begin(b, c, k, kind, slot, device):
        index = 1 if b is None else b
        rows = pl.ds(0, halo) if k is None else pl.ds(k * n_rows, n_rows)
        if b is None and isinstance(c, int):
            source = edge_rows.at[rows]
        else:
            source = out_ref.at[0, index, c, rows]
        k = 0 if k is None else k
        copy = remote(source, out_ref.at[(*slot, rows)], n_send.at[kind, index, c, k], n_receive.at[(*slot, k)], device)
        copy.start()
        started.append(copy)
        return copy

    def landing(a, b, c, k=None):
        rows = pl.ds(0, halo) if k is None else pl.ds(k * n_rows, n_rows)
        there = out_ref.at[a, b, c, rows]
        remote(there, there, n_send.at[0, 0, 0, 0], n_receive.at[a, b, c, 0 if k is None else k], place.first).wait_recv()

    def to_siblings_next(b, c):
        for i, device in enumerate(place.siblings):
            begin(b, c, None, 4 + i, (place.sibling_slot(i), 1 if b is None else b, c), device)

    away = jnp.where(z == nz - 1, 1, -1)
    at_end = (z == 0) | (z == nz - 1)
    for k in range(chunks_next):
        begin(None, 1, k, 0, (0, 1, 0), place.along_z(1))
        begin(None, 1, k, 1, (0, 1, 2), place.along_z(-1))
    to_diagonal = [begin(None, 1, k, 3, (0, place.b_first, 1), place.diagonal) for k in range(chunks_next)]
    for k in range(chunks_next):
        begin(None, 1, k, 2, (0, place.b_second, 1), place.first)
    to_siblings_next(None, 1)
    centre = pltpu.make_async_copy(edge_rows, out_ref.at[0, 1, 1], local.at[0])
    centre.start()
    fresh[...] = new_rows
    keep = pltpu.make_async_copy(fresh, new_ref, local.at[1])
    keep.start()
    for step in range(nz - 1):
        returned(step).wait_send()
    near = jnp.where(z == 0, 2, 0)
    order = (1, near, 2 - near)

    def own_next(c):
        for k in range(chunks_next):
            landing(0, 1, c, k)
            begin(None, c, k, 2, (0, place.b_second, c), place.first)
        to_siblings_next(None, c)

    def other_next(b, c):
        for k in range(chunks_next):
            landing(0, b, c, k)
            if b is place.b_second and isinstance(c, int):
                begin(b, c, k, 0, (0, b, 0), place.along_z(1))
                begin(b, c, k, 1, (0, b, 2), place.along_z(-1))
        to_siblings_next(b, c)

    own_next(order[1])
    other_next(place.b_second, 1)
    own_next(order[2])
    for c in order:
        other_next(place.b_first, c)
    for c in order[1:]:
        other_next(place.b_second, c)
    for b in (1, place.b_first, place.b_second):
        for a in range(1, na):
            for c in order:
                landing(a, b, c)
    for copy in started:
        copy.wait_send()
    keep.wait()
    centre.wait()


def spread_kernel(new_ref, blocks_ref, new_out, out_ref, row_sem, out_sem):
    na = blocks_ref.shape[0]
    parts = (1, 0, 1) if na == 2 else (2, 0, 1)
    stores = [pltpu.make_async_copy(new_ref, new_out, row_sem.at[0])]
    stores[0].start()
    for part, slot in enumerate(parts):
        for b in range(3):
            for c in range(3):
                cell = part * 9 + b * 3 + c
                if cell != 13:
                    cell = cell - 1 if cell > 13 else cell
                    stores.append(pltpu.make_async_copy(blocks_ref.at[slot, b, c], out_ref.at[cell], out_sem.at[cell]))
                    stores[-1].start()
    for copy in stores:
        copy.wait()


def shards(sizes, features, halo_index, edge_src, edge_dst, edge_count, edge_basis, w_edge_in, w_edge_out, w_update):
    nx, ny, nz = sizes
    atoms, width = features.shape
    groups, slots = edge_src.shape
    halo = halo_index.shape[0]
    radial = edge_basis.shape[1]
    hidden = w_edge_in.shape[2]
    lanes = -(-max(atoms, halo) // 128) * 128
    na = 2 if nx == 2 else 3
    f32, bf16 = jnp.float32, jnp.bfloat16
    basis = edge_basis.reshape(groups, slots, radial)
    anywhere = pl.BlockSpec(memory_space=pl.ANY)
    dma = pltpu.SemaphoreType.DMA
    chunks = 1
    pieces = 2
    chunks_next = 1
    meta_rows = -(-(2 * (slots // lanes) + 1) // 8) * 8
    hbm = functools.partial(pltpu.with_memory_space_constraint, memory_space=pltpu.HBM)
    group = na * 3 * halo
    window = -(-3 * group // lanes) * lanes
    table_rows = (nz - 1) * group + window
    new_rows, blocks = pl.pallas_call(
        functools.partial(layer_kernel, sizes),
        out_shape=(
            pltpu.VMEM((atoms, width), bf16),
            pltpu.VMEM((na, 3, 3, halo, width), bf16),
        ),
        in_specs=[anywhere] * 9,
        out_specs=(anywhere, anywhere),
        scratch_shapes=[
            pltpu.VMEM((atoms, width), bf16),
            pltpu.VMEM((1, halo), jnp.int32),
            pltpu.VMEM((groups, slots), jnp.int32),
            pltpu.VMEM((groups, slots), jnp.int32),
            pltpu.SMEM((groups,), jnp.int32),
            pltpu.VMEM((nz, meta_rows, lanes), f32),
            pltpu.VMEM((nz, atoms, width), bf16),
            pltpu.VMEM((nz, slots, radial), bf16),
            pltpu.VMEM((nz, meta_rows, lanes), f32),
            pltpu.VMEM(w_edge_in.shape[1:], bf16),
            pltpu.VMEM(w_edge_out.shape[1:], bf16),
            pltpu.VMEM(w_update.shape, bf16),
            pltpu.VMEM((table_rows, width), bf16),
            pltpu.VMEM((nz, radial + lanes, hidden), bf16),
            pltpu.VMEM((nz - 1, atoms, width), bf16),
            pltpu.VMEM((nz - 1, atoms, width), bf16),
            pltpu.VMEM((halo, width), bf16),
            pltpu.VMEM((atoms, width), bf16),
            dma((2, nz, pieces)),
            dma((nz, pieces)),
            dma((3, nz, chunks)),
            dma((na, 3, nz, chunks)),
            dma((na - 1, 3, nz)),
            dma((2, nz)),
            dma((2, nz)),
            dma((9,)),
            dma((nz - 1,)),
            dma((nz - 1,)),
            dma((4 + na - 1, 3, 3, chunks_next)),
            dma((na, 3, 3, chunks_next)),
        ],
        compiler_params=pltpu.CompilerParams(
            collective_id=0, has_side_effects=True, vmem_limit_bytes=56 * 1024 * 1024
        ),
        name="layer",
    )(*(hbm(array) for array in (features, halo_index.reshape(1, halo), edge_src, edge_dst, edge_count, basis,
                                  w_edge_in[0], w_edge_out[0], w_update)))
    blocks = pltpu.with_memory_space_constraint(blocks, pltpu.VMEM)
    new_rows = pltpu.with_memory_space_constraint(new_rows, pltpu.VMEM)
    return pl.pallas_call(
        spread_kernel,
        out_shape=(
            jax.ShapeDtypeStruct((atoms, width), bf16),
            jax.ShapeDtypeStruct((26, halo, width), bf16),
        ),
        in_specs=[anywhere, anywhere],
        out_specs=(anywhere, anywhere),
        scratch_shapes=[
            dma((1,)),
            dma((26,)),
        ],
        name="spread",
    )(new_rows, blocks)


def solution(mesh):
    sizes = tuple(mesh.shape[name] for name in AXES)
    in_specs = (
        P(AXES, None),
        P(AXES),
        P(AXES, None),
        P(AXES, None),
        P(AXES),
        P(AXES, None),
        P("gz", None, None),
        P("gz", None, None),
        P(),
    )
    out_specs = (P(AXES, None), P(AXES, None, None))
    return jax.shard_map(
        functools.partial(shards, sizes), mesh=mesh, in_specs=in_specs, out_specs=out_specs, check_vma=False
    )
```
